32 devices in a mesh: group: 1, req: 4 (over z), head: 4 (over y, x), pool: 2 (over core).
Axes of the slice: x: 2, y: 2, z: 4, core: 2. Of those that a mesh axis runs over, the one named last changes fastest.
Arguments:
- queries: bfloat16 [192, 4096], P(('group', 'req'), 'head'), may hold values from -128 to 128
- new_entries: bfloat16 [192, 2, 4, 256], P(('group', 'req'), None, 'head'), may hold values from -6 to 6
- cache_pages: bfloat16 [4, 416, 16, 256], P('head', ('group', 'req', 'pool')), may hold values from -6 to 6
- page_table: int32 [192, 2, 1], P(('group', 'req'), 'pool'), may hold values from 0 to 51, as said below
- cached_length: int32 [192, 2], P(('group', 'req'), 'pool'), may hold values from 1 to 16, as said below
- leave_slots: int32 [32], P(('group', 'req', 'pool')), may hold values from 0 to 50, as said below
- arrive_slots: int32 [32], P(('group', 'req', 'pool')), may hold values from 0 to 51, as said below
- residual: bfloat16 [192, 2048], P(('group', 'req', 'head')), may hold values from -5 to 5
- norm_gain: float32 [2048], replicated, may hold values from 0.5 to 1.5
- output_weight: bfloat16 [4096, 2048], P(('head', 'pool')), may hold values from -0.25 to 0.25
- expert_choice: int32 [192, 8], P(('group', 'req', 'head')), may hold values from 0 to 15, all different within a row; in each aligned block of 12 rows (0 to 11, 12 to 23, ...) at most 12 rows name the same one
- route_weight: float32 [192, 8], P(('group', 'req', 'head')), may hold values from 0.2 to 1
- gate_up: bfloat16 [16, 2, 384, 2048], P(('req', 'head'), None, 'pool'), may hold values from -0.125 to 0.125
- down_weight: bfloat16 [16, 384, 2048], P(('req', 'head'), 'pool'), may hold values from -0.3125 to 0.3125
Outputs:
- decoded: bfloat16 [192, 2048], P(('group', 'req', 'head'), 'pool')
The draws below stay inside these ranges and needn't reach their ends.
Inputs may be any that keep to these rules, and one draw needn't show every extreme that they name: `page_table`: within each block of one index of req and one pool, the 48 entries name distinct slots, none of them among that block's leave_slots. `leave_slots`: each block's 4 entries are distinct. `arrive_slots`: each block's 4 entries are distinct slots that its page table names. `cached_length`: in every block of 48 requests and each pool some request has 16. `expert_choice`: each row names 8 distinct experts; in each aligned block of 12 rows no expert is named more than 12 times, a bound that some block reaches.
All inputs are finite; a program needn't handle non-finite values.
Results may differ from the reference program's by a relative error of at most 0.023.
Values may be sent and summed in bfloat16 or wider, within the bound.
A program may use at most 64 MiB of HBM per device.

```python
import math
import jax
import jax.numpy as jnp
import numpy as np
from jax import lax

D = 2048
HEADS = 32
KVH = 4
HEAD_SIZE = 128
TOPK = 8
FF_E = 384
B_DEV = 48
PAGE = 16
PPR = 1
MOVE = 4
SLOT_DEV = 52
SLOTS = 416
REQS = 192
RD = 12
EXPERTS = 16
CAP = 12
N_REQ = 4
N_POOL = 2


def paging(key):
    used_count = B_DEV * PPR
    base_key = jax.random.fold_in(key, 7001)

    def single(device_key):
        first_key, second_key, third_key = jax.random.split(device_key, 3)
        base_order = jax.random.permutation(first_key, SLOT_DEV - 2).astype(jnp.int32)
        leaving = jnp.concatenate([jnp.full((1,), SLOT_DEV - 2, jnp.int32), base_order[:MOVE - 1]])
        others = base_order[MOVE - 1:]
        table_rows = jnp.concatenate([jnp.full((1,), SLOT_DEV - 1, jnp.int32), others])
        table_rows = table_rows[jax.random.permutation(second_key, used_count)]
        picked = others[jax.random.permutation(third_key, used_count - 1)[:MOVE - 1]]
        arriving = jnp.concatenate([jnp.full((1,), SLOT_DEV - 1, jnp.int32), picked])
        return (table_rows.reshape(B_DEV, PPR), leaving, arriving)
    tables, leaving, arriving = jax.vmap(single)(jax.random.split(base_key, N_REQ * N_POOL))
    tables = tables.reshape(N_REQ, N_POOL, B_DEV, PPR).transpose(0, 2, 1, 3).reshape(N_REQ * B_DEV, N_POOL, PPR)
    return (tables.astype(jnp.int32), leaving.reshape(-1).astype(jnp.int32), arriving.reshape(-1).astype(jnp.int32))


def draw_page_table(key, part):
    return paging(key)[0]


def draw_leave_slots(key, part):
    return paging(key)[1]


def draw_arrive_slots(key, part):
    return paging(key)[2]


def draw_cached_length(key, part):
    first_key, second_key = jax.random.split(jax.random.fold_in(key, 7002))
    longest = PPR * PAGE
    lengths = jax.random.randint(first_key, (N_REQ, B_DEV, N_POOL), 1, longest + 1)
    chosen = jax.random.randint(second_key, (N_REQ, 1, N_POOL), 0, B_DEV)
    at_most = jnp.arange(B_DEV)[None, :, None] == chosen
    return jnp.where(at_most, longest, lengths).reshape(N_REQ * B_DEV, N_POOL).astype(jnp.int32)


def attention_draw(key):
    split_keys = jax.random.split(jax.random.fold_in(key, 7003), 2)
    total_rows = N_REQ * B_DEV
    group_size = HEADS // KVH
    queries = jnp.clip(jax.random.normal(split_keys[0], (total_rows, KVH, group_size, HEAD_SIZE), jnp.float32), -6.0, 6.0)
    entries = jnp.clip(jax.random.normal(split_keys[1], (total_rows, 2, KVH, 2 * HEAD_SIZE), jnp.float32), -6.0, 6.0)
    return (queries.reshape(total_rows, HEADS * HEAD_SIZE), entries)


def draw_queries(key, part):
    return attention_draw(key)[0].astype(jnp.bfloat16)


def draw_new_entries(key, part):
    return attention_draw(key)[1].astype(jnp.bfloat16)


def draw_residual(key, part):
    first_key = jax.random.fold_in(jax.random.fold_in(key, 7004), 0)
    total_rows = N_REQ * B_DEV
    values = jnp.clip(jax.random.normal(first_key, (total_rows, D), jnp.float32), -6.0, 6.0) * 0.5
    return values.astype(jnp.bfloat16)


def block_scale(key, shape, cuts, smallest, largest):
    level, own = 1.0, jax.random.fold_in(key, 6)
    for axis_at, blocks in cuts:
        steps = jnp.exp(jax.random.uniform(jax.random.fold_in(own, axis_at), (blocks,), jnp.float32, smallest / len(cuts), largest / len(cuts)))
        level = level * jnp.repeat(steps, shape[axis_at] // blocks).reshape([-1 if axis == axis_at else 1 for axis in range(len(shape))])
    return level


def routed_block(stream_key, own, number, rows, count, top, limit, lean):
    sequence = jax.random.permutation(stream_key, count)
    crowded, usual = load_shares(count, rows * top, limit, lean, True), load_shares(count, rows * top, limit, lean, False)
    places = jnp.arange(count)

    def named(sizes, rotation):
        used = int((sizes > 0).sum())
        fixed = max(1, used // 4)
        moved = fixed + (places - fixed + rotation * (used - fixed)) % max(1, count - fixed)
        return jnp.zeros((count,), jnp.int32).at[sequence[jnp.where(places < fixed, places, moved)]].set(jnp.asarray(sizes, jnp.int32))

    sizes = jnp.where(number % 4 == 0, named(crowded, number // 4), named(usual, number - number // 4 - 1))
    mixed = jax.random.permutation(jax.random.fold_in(own, 3), count)
    source_of, sink = mixed[0:count // 2 * 2:2], mixed[1:count // 2 * 2:2]
    room = jnp.minimum(sizes[source_of] - 1, limit - sizes[sink]) // 2
    room = jnp.where((source_of == sequence[0]) | (sink == sequence[0]) | (sizes[sink] == 0), 0, jnp.maximum(room, 0))
    moved = jax.random.randint(jax.random.fold_in(own, 4), (count // 2,), 0, 1 << 20) % (room + 1)
    sizes = sizes.at[source_of].add(-moved).at[sink].add(moved)
    members = jnp.searchsorted(jnp.cumsum(sizes), jnp.arange(rows * top), side="right").astype(jnp.int32)
    grid = members.reshape(top, rows).T
    grid = grid[jax.random.permutation(jax.random.fold_in(own, 1), rows)]
    rotation = jax.random.randint(jax.random.fold_in(own, 2), (rows, 1), 0, top)
    return jnp.take_along_axis(grid, (jnp.arange(top)[None, :] + rotation) % top, axis=1)


def load_shares(number_of, total, reach, slope, full):
    loads = [(1 << 20) // math.isqrt(rank ** slope) + 1 for rank in range(1, number_of + 1)]
    largest = reach if full else min(reach, max(-(-total // number_of), total * loads[0] // sum(loads)))
    least = 1 if total - largest >= number_of - 1 else 0
    given, rest = [largest] + [least] * (number_of - 1), total - largest - least * (number_of - 1)
    while rest > 0:
        movable = [i for i in range(1, number_of) if given[i] < largest] or [i for i in range(1, number_of) if given[i] < reach]
        mass, left = sum([loads[i] for i in movable]), rest
        for i in movable:
            extra = min(reach - given[i], max(1, left * loads[i] // mass), rest)
            given[i] = given[i] + extra
            rest = rest - extra
    return np.array(given)


def normal_values(own_key, shape, scale, bound, cuts=(), held_as=jnp.bfloat16):
    loudness = block_scale(own_key, shape, cuts, -0.22, 0.18) if cuts else 1.0
    values = jax.random.normal(own_key, shape, jnp.float32) * scale * loudness
    return jnp.minimum(jnp.maximum(values, -bound), bound).astype(held_as)


def setup_inputs(seed: int = 0, part: int = 0) -> dict:
    arg_keys = jax.random.split(jax.random.key(seed), 15)
    part_splits = jax.random.split(jax.random.fold_in(arg_keys[14], part), 15)
    queries = draw_queries(jax.random.fold_in(jax.random.fold_in(arg_keys[14], part), 71), part)
    new_entries = draw_new_entries(jax.random.fold_in(jax.random.fold_in(arg_keys[14], part), 71), part)
    cache_pages = normal_values(part_splits[2], (KVH, SLOTS, PAGE, 2 * HEAD_SIZE), 1.0, 6.0, ((0, 4), (1, 8)))
    page_table = draw_page_table(jax.random.fold_in(jax.random.fold_in(arg_keys[14], part), 71), part)
    cached_length = draw_cached_length(jax.random.fold_in(jax.random.fold_in(arg_keys[14], part), 71), part)
    leave_slots = draw_leave_slots(jax.random.fold_in(jax.random.fold_in(arg_keys[14], part), 71), part)
    arrive_slots = draw_arrive_slots(jax.random.fold_in(jax.random.fold_in(arg_keys[14], part), 71), part)
    residual = draw_residual(jax.random.fold_in(jax.random.fold_in(arg_keys[14], part), 71), part)
    norm_gain = jnp.clip(1.0 + 0.1 * jax.random.normal(arg_keys[8], (D,), jnp.float32), 0.5, 1.5)
    output_weight = normal_values(arg_keys[9], (HEADS * HEAD_SIZE, D), (HEADS * HEAD_SIZE // 8) ** -0.5, 0.25, ((0, 8),))
    expert_choice_keys = jax.random.split(jax.random.fold_in(part_splits[10], 1), REQS // RD)
    expert_choice_turns = jax.random.permutation(jax.random.fold_in(part_splits[10], 3), REQS // RD)
    expert_choice = jax.vmap(lambda own, number: routed_block(jax.random.fold_in(part_splits[10], 2), own, number, RD, EXPERTS, TOPK, CAP, 2))(expert_choice_keys, expert_choice_turns).reshape((REQS, TOPK))
    route_weight = jnp.clip(0.2 + 0.8 * jax.random.uniform(part_splits[11], (REQS, TOPK), jnp.float32) ** block_scale(part_splits[11], (REQS, TOPK), ((0, 16),), -0.2, 0.2), 0.2, 1.0)
    gate_up = normal_values(arg_keys[12], (EXPERTS, 2, FF_E, D), D ** -0.5, 0.125, ((0, 16), (2, 2)))
    down_weight = normal_values(arg_keys[13], (EXPERTS, FF_E, D), FF_E ** -0.5, 0.3125, ((0, 16), (1, 2)))
    return dict(queries=queries, new_entries=new_entries, cache_pages=cache_pages, page_table=page_table, cached_length=cached_length, leave_slots=leave_slots, arrive_slots=arrive_slots, residual=residual, norm_gain=norm_gain, output_weight=output_weight, expert_choice=expert_choice, route_weight=route_weight, gate_up=gate_up, down_weight=down_weight)


def reference(queries, new_entries, cache_pages, page_table, cached_length, leave_slots, arrive_slots, residual, norm_gain, output_weight, expert_choice, route_weight, gate_up, down_weight):
    slot_count = B_DEV * PPR + MOVE
    total_rows = N_REQ * B_DEV
    group_size = HEADS // KVH
    page_store = cache_pages.reshape(KVH, N_REQ, N_POOL, slot_count, PAGE, 2 * HEAD_SIZE)
    leaving = leave_slots.reshape(N_REQ, N_POOL, MOVE)
    arriving = arrive_slots.reshape(N_REQ, N_POOL, MOVE)
    req_index = jnp.arange(N_REQ, dtype=jnp.int32)[:, None, None]
    pool_index = jnp.arange(N_POOL, dtype=jnp.int32)[None, :, None]
    moved_pages = page_store[:, req_index, 1 - pool_index, leaving[:, ::-1, :]]
    page_store = page_store.at[:, req_index, pool_index, arriving].set(moved_pages)
    owner_index = (jnp.arange(total_rows, dtype=jnp.int32) // B_DEV)[:, None, None]
    positions = jnp.arange(PPR * PAGE, dtype=jnp.int32)
    valid_mask = (positions[None, None, :] < cached_length[:, :, None]).reshape(total_rows, N_POOL * PPR * PAGE)
    valid_mask = jnp.concatenate([valid_mask, jnp.ones((total_rows, 2), dtype=bool)], axis=1)
    grouped_queries = queries.astype(jnp.float32).reshape(total_rows, KVH, group_size, HEAD_SIZE)
    newest = new_entries.astype(jnp.float32)

    def one_group(query_group_index):
        context = page_store[query_group_index][owner_index, pool_index, page_table]
        context = context.reshape(total_rows, N_POOL * PPR * PAGE, 2 * HEAD_SIZE).astype(jnp.float32)
        entries = jnp.concatenate([context, newest[:, :, query_group_index, :]], axis=1)
        paged_key_rows = entries[:, :, :HEAD_SIZE]
        paged_value_rows = entries[:, :, HEAD_SIZE:]
        attention_scores = jnp.einsum('xsw,xlw->xsl', grouped_queries[:, query_group_index], paged_key_rows) * HEAD_SIZE ** (-0.5)
        attention_scores = jnp.where(valid_mask[:, None, :], attention_scores, -jnp.inf)
        attention_weights = jax.nn.softmax(attention_scores, axis=-1)
        return jnp.einsum('usj,ujw->usw', attention_weights, paged_value_rows)
    attended = lax.map(one_group, jnp.arange(KVH, dtype=jnp.int32))
    attended = attended.transpose(1, 0, 2, 3).reshape(total_rows, HEADS * HEAD_SIZE).astype(jnp.bfloat16)
    attention = jnp.dot(attended, output_weight, preferred_element_type=jnp.float32)
    hidden = residual.astype(jnp.float32) + attention
    normed = (hidden * lax.rsqrt(lax.optimization_barrier(jnp.mean(hidden * hidden, axis=-1, keepdims=True)) + 1e-06) * norm_gain.astype(jnp.float32)).astype(jnp.bfloat16)
    capacity = EXPERTS * CAP
    row_ids = jnp.arange(total_rows, dtype=jnp.int32)

    def one_expert(accumulated, expert):
        expert_hits = expert_choice == expert
        weight = lax.optimization_barrier(jnp.sum(jnp.where(expert_hits, route_weight.astype(jnp.float32), 0.0), axis=1))
        chosen = jnp.any(expert_hits, axis=1)
        ranking = jnp.where(chosen, total_rows - row_ids, 0).astype(jnp.int32)
        top_values, picked = lax.top_k(ranking, capacity)
        picked = picked.astype(jnp.int32)
        inputs = normed[picked]
        projected = jnp.dot(inputs, gate_up[expert].reshape(2 * FF_E, D).T, preferred_element_type=jnp.float32)
        activated = (jax.nn.silu(projected[:, :FF_E]) * projected[:, FF_E:]).astype(jnp.bfloat16)
        output = jnp.dot(activated, down_weight[expert], preferred_element_type=jnp.float32).astype(jnp.bfloat16)
        contribution = weight[picked][:, None] * output.astype(jnp.float32)
        return (accumulated.at[picked].add(contribution), None)
    mixture, unused = lax.scan(one_expert, jnp.zeros((total_rows, D), jnp.float32), jnp.arange(EXPERTS, dtype=jnp.int32))
    return (hidden + mixture).astype(jnp.bfloat16)
```

```python
import functools

import jax
import jax.numpy as jnp
from jax import lax
from jax.experimental import pallas as pl
from jax.experimental.pallas import tpu as pltpu
from jax.sharding import PartitionSpec as P

MESH = pl.DeviceIdType.MESH
ROW_TILE = 16
NEGATIVE = -1e30


def swapped(value, axis, apart):
    mask = 2**apart
    pairs = [(source, source ^ mask) for source in range(lax.axis_size(axis))]
    return lax.ppermute(value, axis, pairs)


def combined_all(shard, axis, join):
    gathered = jax.tree.map(
        lambda a, kind: lax.all_gather(a.astype(kind), axis),
        shard,
        (jnp.bfloat16, jnp.bfloat16, jnp.bfloat16),
    )

    def take(source):
        return jax.tree.map(
            lambda a, own: lax.dynamic_index_in_dim(a, source, 0, False).astype(own.dtype),
            gathered,
            shard,
        )

    return lax.fori_loop(
        1, lax.axis_size(axis), lambda source, state: join(state, take(source)), take(0)
    )


def merge_parts(earlier, later):
    first_max, first_denominator, first_value = earlier
    second_max, second_denominator, second_value = later
    largest = jnp.maximum(first_max, second_max)
    first_scale = jnp.exp(first_max - largest)
    second_scale = jnp.exp(second_max - largest)
    denominator = first_denominator * first_scale + second_denominator * second_scale
    weighted = first_value * first_scale[..., None] + second_value * second_scale[..., None]
    return (largest, denominator, weighted)


def local_routed(
    queries,
    new_entries,
    cache_pages,
    page_table,
    cached_length,
    leave_slots,
    arrive_slots,
    residual,
    norm_gain,
    output_weight,
    expert_choice,
    route_weight,
    gate_up,
    down_weight,
):
    batch_size = queries.shape[0]
    group_count = cache_pages.shape[0]
    head_dim = new_entries.shape[3] // 2
    group_size = queries.shape[1] // (group_count * head_dim)
    pool_index = lax.axis_index("pool")
    outgoing = cache_pages[:, leave_slots]
    arrived = swapped(outgoing, "pool", 0)
    current = cache_pages.at[:, arrive_slots].set(arrived)
    context = current[:, page_table[:, 0, :]]
    context = context.reshape(group_count, batch_size, -1, 2 * head_dim)
    context_keys = context[..., :head_dim]
    context_values = context[..., head_dim:]
    grouped_queries = queries.reshape(batch_size, group_count, group_size, head_dim)
    score_scale = head_dim ** (-0.5)
    attention_scores = (
        jnp.einsum(
            "bgqd,gbtd->bgqt", grouped_queries, context_keys, preferred_element_type=jnp.float32
        )
        * score_scale
    )
    positions = jnp.arange(context.shape[2], dtype=jnp.int32)
    valid_mask = positions[None, :] < cached_length
    attention_scores = jnp.where(valid_mask[:, None, None, :], attention_scores, -jnp.inf)
    fresh_scores = (
        jnp.einsum(
            "bgqd,bsgd->bgqs",
            grouped_queries,
            new_entries[..., :head_dim],
            preferred_element_type=jnp.float32,
        )
        * score_scale
    )
    fresh_scores = jnp.where(pool_index == 0, fresh_scores, -jnp.inf)
    largest = jnp.maximum(jnp.max(attention_scores, axis=-1), jnp.max(fresh_scores, axis=-1))
    local_weights = jnp.exp(attention_scores - largest[..., None])
    fresh_weights = jnp.exp(fresh_scores - largest[..., None])
    denominator = jnp.sum(local_weights, axis=-1) + jnp.sum(fresh_weights, axis=-1)
    weighted = jnp.einsum("bgqt,gbtd->bgqd", local_weights, context_values.astype(jnp.float32))
    weighted = weighted + jnp.einsum(
        "bgqs,bsgd->bgqd", fresh_weights, new_entries[..., head_dim:].astype(jnp.float32)
    )
    largest, denominator, weighted = combined_all(
        (largest, denominator, weighted), "pool", merge_parts
    )
    attended = (weighted / denominator[..., None]).reshape(batch_size, -1).astype(jnp.bfloat16)
    head_width = output_weight.shape[0]
    own_heads = lax.dynamic_slice_in_dim(attended, pool_index * head_width, head_width, 1)
    partial_value = jnp.dot(own_heads, output_weight, preferred_element_type=jnp.float32)
    rows_here = residual.shape[0]
    summed = lax.psum(partial_value.astype(jnp.bfloat16), ("head", "pool")).astype(jnp.float32)
    attention = lax.dynamic_slice_in_dim(summed, lax.axis_index("head") * rows_here, rows_here, 0)
    hidden = residual.astype(jnp.float32) + attention
    normed = (
        hidden * lax.rsqrt(jnp.mean(hidden * hidden, axis=-1, keepdims=True) + 1e-06) * norm_gain
    ).astype(jnp.bfloat16)
    expert_count = lax.axis_size("req") * lax.axis_size("head")
    top_count = expert_choice.shape[1]
    capacity = max(
        2, min(rows_here, (2 * rows_here * top_count + expert_count - 1) // expert_count)
    )
    flat_choice = expert_choice.reshape(-1)
    expert_hits = (
        flat_choice[:, None] == jnp.arange(expert_count, dtype=jnp.int32)[None, :]
    ).astype(jnp.int32)
    earlier = jnp.cumsum(expert_hits, axis=0) - expert_hits
    slot_index = jnp.sum(earlier * expert_hits, axis=1)
    target = flat_choice * capacity + slot_index
    placed = (
        target[:, None] == jnp.arange(expert_count * capacity, dtype=jnp.int32)[None, :]
    ).astype(jnp.float32)
    placed = placed.reshape(rows_here, top_count, expert_count * capacity)
    dispatch = jnp.sum(placed, axis=1).astype(jnp.bfloat16)
    combine_matrix = jnp.sum(placed * route_weight[:, :, None], axis=1)
    outgoing_rows = jnp.einsum("re,rd->ed", dispatch, normed, preferred_element_type=jnp.float32)
    outgoing_rows = outgoing_rows.astype(jnp.bfloat16).reshape(expert_count, capacity, -1)
    model_width = normed.shape[1]
    half_width = model_width // lax.axis_size("pool")
    projection = gate_up[0].reshape(-1, model_width)
    hidden_size = projection.shape[0] // 2
    received = lax.all_to_all(
        outgoing_rows, ("req", "head"), split_axis=0, concat_axis=0, tiled=True
    )
    sources = received.shape[0]
    item_count = received.shape[1]
    flat_rows = received.reshape(sources * item_count, model_width)
    projected = jnp.einsum("nd,fd->nf", flat_rows, projection, preferred_element_type=jnp.float32)
    activated = (jax.nn.silu(projected[:, :hidden_size]) * projected[:, hidden_size:]).astype(
        jnp.bfloat16
    )
    part_sum = jnp.dot(activated, down_weight[0], preferred_element_type=jnp.float32).reshape(
        sources, item_count, model_width
    )
    column_sum = lax.psum_scatter(
        part_sum.astype(jnp.bfloat16), "pool", scatter_dimension=2, tiled=True
    )
    returned = lax.all_to_all(column_sum, ("req", "head"), split_axis=0, concat_axis=0, tiled=True)
    gathered = returned.reshape(expert_count * capacity, half_width).astype(jnp.float32)
    expert_mix = jnp.dot(combine_matrix, gathered, precision=lax.Precision.HIGHEST)
    own_columns = lax.dynamic_slice_in_dim(hidden, pool_index * half_width, half_width, 1)
    return (own_columns + expert_mix).astype(jnp.bfloat16)


def layer_kernel(
    req_count,
    head_count,
    pool_count,
    page_table,
    leave_slots,
    arrive_slots,
    cached_length,
    expert_choice,
    route_weight,
    residual,
    norm_gain,
    queries_hbm,
    fresh_hbm,
    cache_hbm,
    output_weight_hbm,
    gate_up_hbm,
    down_weight_hbm,
    decoded,
    queries,
    fresh,
    cache,
    output_weight,
    gate_up,
    down_weight,
    leaving,
    arrived,
    context,
    weights,
    values_out,
    values_in,
    level_out,
    level_in,
    partial_out,
    partial_in,
    hidden,
    active,
    own_part,
    pool_out,
    pool_in,
    head_out,
    head_in,
    totals,
    req_out,
    req_in,
    load_sem,
    send_sem,
    recv_sem,
):
    r, h, p = lax.axis_index("req"), lax.axis_index("head"), lax.axis_index("pool")
    batch, page = queries.shape[0], cache.shape[1]
    head_dim = cache.shape[2] // 2
    group_size = queries.shape[1] // head_dim
    rows_here = residual.shape[0]
    width = residual.shape[1]
    col_block = width // (head_count * pool_count)
    half = width // pool_count
    half_heads = group_size // pool_count
    chunks = batch // ROW_TILE
    moves = leaving.shape[0]

    loads = [
        pltpu.make_async_copy(source, target, load_sem.at[i])
        for i, (source, target) in enumerate(
            (
                (cache_hbm.at[0], cache),
                (queries_hbm, queries),
                (fresh_hbm.at[p], fresh),
                (output_weight_hbm, output_weight),
                (gate_up_hbm.at[0], gate_up),
                (down_weight_hbm.at[0], down_weight),
            )
        )
    ]
    for load in loads:
        load.start()

    def req_peer(k):
        return lax.rem(r + k, req_count)

    def head_peer(k):
        return lax.rem(h + k, head_count)

    def req_source(k):
        return lax.rem(r + req_count - k, req_count)

    def head_source(k):
        return lax.rem(h + head_count - k, head_count)

    partner = 1 - p
    barrier = pltpu.get_barrier_semaphore()
    peers = [
        (kr, kh, kp)
        for kr in range(req_count)
        for kh in range(head_count)
        for kp in range(pool_count)
        if (kr, kh, kp) != (0, 0, 0) and (kp == 0 or kr == 0)
    ]

    def where_is(kr, kh, kp):
        return {
            "req": req_peer(kr) if kr else r,
            "head": head_peer(kh) if kh else h,
            "pool": partner if kp else p,
        }

    for peer in peers:
        pl.semaphore_signal(barrier, inc=1, device_id=where_is(*peer), device_id_type=MESH)

    lane = lax.broadcasted_iota(jnp.int32, (rows_here, weights.shape[2]), 1)
    dense = jnp.zeros((rows_here, weights.shape[2]), jnp.float32)
    for k in range(expert_choice.shape[1]):
        dense = dense + jnp.where(lane == expert_choice[:, k : k + 1], route_weight[:, k : k + 1], 0.0)
    own_block = h * req_count + r
    weights[own_block] = jnp.concatenate(
        [dense, jnp.zeros((ROW_TILE - rows_here, weights.shape[2]), jnp.float32)], axis=0
    )

    sent = []

    def send(source, target, kr, kh, kp):
        at = len(sent)
        copy = pltpu.make_async_remote_copy(
            src_ref=source,
            dst_ref=target,
            send_sem=send_sem.at[at],
            recv_sem=recv_sem.at[at],
            device_id=where_is(kr, kh, kp),
            device_id_type=MESH,
        )
        copy.start()
        sent.append(copy)
        return copy

    loads[0].wait()
    for k in range(moves):
        leaving[k] = cache[leave_slots[k]]
    pl.semaphore_wait(barrier, len(peers))
    pages = send(leaving, arrived, 0, 0, 1)
    weight_copies = [
        send(weights.at[own_block], weights.at[own_block], kr, kh, 0)
        for kr in range(req_count)
        for kh in range(head_count)
        if kr or kh
    ]
    loads[1].wait()
    loads[2].wait()
    pages.wait_recv()

    def gather(b, carry):
        slot = page_table[b]
        which, moved = jnp.int32(0), jnp.int32(0)
        for k in range(moves):
            hit = arrive_slots[k] == slot
            which = jnp.where(hit, k, which)
            moved = jnp.where(hit, 1, moved)
        flag = jnp.full((page, 2 * head_dim), moved, jnp.int32) > 0
        kept = cache[slot].astype(jnp.float32)
        swapped_in = arrived[which].astype(jnp.float32)
        context[b] = jnp.where(flag, swapped_in, kept).astype(jnp.bfloat16)
        return carry

    lax.fori_loop(0, batch, gather, 0, unroll=8)

    tile_rows = group_size * ROW_TILE
    score_scale = head_dim ** (-0.5)
    for c in range(chunks):
        base = c * ROW_TILE
        stacked = jnp.concatenate(
            [
                queries[base : base + ROW_TILE, g * head_dim : (g + 1) * head_dim]
                for g in range(group_size)
            ],
            axis=0,
        )
        block = context[base : base + ROW_TILE].reshape(ROW_TILE * page, 2 * head_dim)
        scores = (
            lax.dot_general(
                stacked,
                block[:, :head_dim],
                (((1,), (1,)), ((), ())),
                preferred_element_type=jnp.float32,
            )
            * score_scale
        )
        shape = (ROW_TILE, ROW_TILE * page)
        first = lax.broadcasted_iota(jnp.int32, shape, 0) * page
        offset = lax.broadcasted_iota(jnp.int32, shape, 1) - first
        live = (offset >= 0) & (offset < cached_length[base : base + ROW_TILE, :])
        bias = jnp.where(live, 0.0, NEGATIVE)
        bias = jnp.concatenate([bias] * group_size, axis=0)
        scores = jnp.where(bias < 0.0, NEGATIVE, scores)
        newest = fresh[base : base + ROW_TILE, :].astype(jnp.float32)
        newest = jnp.concatenate([newest] * group_size, axis=0)
        fresh_score = (
            jnp.sum(stacked.astype(jnp.float32) * newest[:, :head_dim], axis=-1, keepdims=True)
            * score_scale
        )
        largest = jnp.maximum(jnp.max(scores, axis=-1, keepdims=True), fresh_score)
        raised = jnp.exp(scores - largest)
        fresh_raised = jnp.exp(fresh_score - largest)
        denominator = jnp.sum(raised, axis=-1, keepdims=True) + fresh_raised
        value = jnp.dot(
            raised.astype(jnp.bfloat16), block[:, head_dim:], preferred_element_type=jnp.float32
        )
        value = (value + fresh_raised * newest[:, head_dim:]) / denominator
        level = jnp.broadcast_to(largest + jnp.log(denominator), (tile_rows, head_dim))
        for s in range(pool_count):
            rows = slice(s * half_heads * ROW_TILE, (s + 1) * half_heads * ROW_TILE)
            values_out[s, c] = value[rows].astype(jnp.bfloat16)
            level_out[s, c] = level[rows]
    value_copy = send(values_out.at[partner], values_in, 0, 0, 1)
    level_copy = send(level_out.at[partner], level_in, 0, 0, 1)

    spread = lax.broadcasted_iota(jnp.int32, (batch, rows_here), 0) == (
        lax.broadcasted_iota(jnp.int32, (batch, rows_here), 1) + h * rows_here
    )
    spread = jnp.where(p == 0, spread.astype(jnp.float32), 0.0).astype(jnp.bfloat16)
    loads[3].wait()
    value_copy.wait_recv()
    level_copy.wait_recv()
    merged = []
    for c in range(chunks):
        first_level, second_level = level_out[p, c], level_in[c]
        top = jnp.maximum(first_level, second_level)
        first_share = jnp.exp(first_level - top)
        second_share = jnp.exp(second_level - top)
        value = values_out[p, c].astype(jnp.float32) * first_share
        value = value + values_in[c].astype(jnp.float32) * second_share
        value = (value / (first_share + second_share)).astype(jnp.bfloat16)
        merged.append(
            jnp.concatenate(
                [value[g * ROW_TILE : (g + 1) * ROW_TILE] for g in range(half_heads)], axis=1
            )
        )
    merged = jnp.concatenate(merged, axis=0)
    blocks = head_count * pool_count
    for d in range(blocks):
        columns = slice(d * col_block, (d + 1) * col_block)
        part = jnp.dot(merged, output_weight[:, columns], preferred_element_type=jnp.float32)
        part = part + jnp.dot(spread, residual[:, columns], preferred_element_type=jnp.float32)
        partial_out[d] = part.astype(jnp.bfloat16)
    partial_copies = []
    for kh in list(range(1, head_count)) + [0]:
        for kp in range(pool_count):
            if kh or kp:
                to_pool = partner if kp else p
                to_head = head_peer(kh) if kh else h
                partial_copies.append(
                    send(
                        partial_out.at[to_pool * head_count + to_head],
                        partial_in.at[kh * pool_count + kp],
                        0,
                        kh,
                        kp,
                    )
                )
    mine = p * head_count + h
    summed = partial_out[mine].astype(jnp.float32)
    order = [kh * pool_count + kp for kh in list(range(1, head_count)) + [0] for kp in range(pool_count) if kh or kp]
    for copy, slot in zip(partial_copies, order):
        copy.wait_recv()
        summed = summed + partial_in[slot].astype(jnp.float32)
    hidden[mine, r] = summed.astype(jnp.bfloat16)

    def hidden_block(at_head, at_req):
        return hidden.at[p * head_count + at_head, at_req]

    own_hidden = hidden_block(h, r)
    req_copies = {kr: send(own_hidden, own_hidden, kr, 0, 0) for kr in range(1, req_count)}
    head_copies, pool_copies = {}, {}
    for kh in range(1, head_count):
        head_copies[kh, 0] = send(own_hidden, own_hidden, 0, kh, 0)
    pool_copies[0, 0] = send(own_hidden, own_hidden, 0, 0, 1)
    for kr in range(1, req_count):
        req_copies[kr].wait_recv()
        block = hidden_block(h, req_source(kr))
        for kh in range(1, head_count):
            head_copies[kh, kr] = send(block, block, 0, kh, 0)
        pool_copies[0, kr] = send(block, block, 0, 0, 1)

    loads[4].wait()
    row_count = req_count * batch
    units = gate_up.shape[1]
    gate = jnp.zeros((row_count, units), jnp.float32)
    up = jnp.zeros((row_count, units), jnp.float32)
    squares = jnp.zeros((row_count, 1), jnp.float32)

    def accumulate(state, chunk):
        gate, up, squares = state
        x = hidden[chunk].reshape(row_count, col_block).astype(jnp.float32)
        columns = pl.ds(pl.multiple_of(chunk * col_block, col_block), col_block)
        scaled = (x * norm_gain[:, columns]).astype(jnp.bfloat16)
        contract = (((1,), (1,)), ((), ()))
        gate = gate + lax.dot_general(
            scaled, gate_up[0, :, columns], contract, preferred_element_type=jnp.float32
        )
        up = up + lax.dot_general(
            scaled, gate_up[1, :, columns], contract, preferred_element_type=jnp.float32
        )
        return gate, up, squares + jnp.sum(x * x, axis=-1, keepdims=True)

    state = (gate, up, squares)
    state = accumulate(state, mine)
    for kh in range(1, head_count):
        for kr in range(req_count):
            head_copies[kh, kr].wait_recv()
            block = hidden_block(head_source(kh), req_source(kr) if kr else r)
            pool_copies[kh, kr] = send(block, block, 0, 0, 1)
        state = accumulate(state, p * head_count + head_source(kh))
    for kh in range(head_count):
        for kr in range(req_count):
            pool_copies[kh, kr].wait_recv()
        state = accumulate(state, partner * head_count + (head_source(kh) if kh else h))
    gate, up, squares = state
    scale = lax.rsqrt(squares * (1.0 / width) + 1e-06)
    gate = gate * scale
    activated = (gate / (1.0 + jnp.exp(-gate)) * (up * scale)).astype(jnp.bfloat16)
    place_row = lax.broadcasted_iota(jnp.int32, (ROW_TILE, row_count), 0)
    place_col = lax.broadcasted_iota(jnp.int32, (ROW_TILE, row_count), 1)
    for copy in weight_copies:
        copy.wait_recv()
    for to_head in range(head_count):
        placing = jnp.concatenate(
            [
                (
                    (place_row + (to_req * batch + to_head * rows_here) == place_col)
                    & (place_row < rows_here)
                )
                .astype(jnp.float32)
                .astype(jnp.bfloat16)
                for to_req in range(req_count)
            ],
            axis=0,
        )
        active[to_head] = jnp.dot(placing, activated, preferred_element_type=jnp.float32).astype(
            jnp.bfloat16
        )
    loads[5].wait()
    expert = r * head_count + h
    group_rows = req_count * ROW_TILE

    def expert_part(to_head, side):
        table = weights[pl.ds(to_head * req_count, req_count)].reshape(group_rows, -1)
        spot = lax.broadcasted_iota(jnp.int32, table.shape, 1)
        weight = jnp.sum(jnp.where(spot == expert, table, 0.0), axis=-1, keepdims=True)
        columns = pl.ds(pl.multiple_of(side * half, half), half)
        value = jnp.dot(
            active[to_head], down_weight[:, columns], preferred_element_type=jnp.float32
        )
        return value * weight

    turn = list(range(1, head_count)) + [0]
    swap_copies = {}
    for kh in turn:
        pool_out[kh] = expert_part(head_peer(kh) if kh else h, partner).astype(jnp.bfloat16)
        swap_copies[kh] = send(pool_out.at[kh], pool_in.at[kh], 0, 0, 1)
    for kh in turn:
        own_part[kh] = expert_part(head_peer(kh) if kh else h, p)
    back_copies = []
    for kh in turn:
        swap_copies[kh].wait_recv()
        both = own_part[kh] + pool_in[kh].astype(jnp.float32)
        if kh:
            head_out[kh - 1] = both.astype(jnp.bfloat16)
            back_copies.append(send(head_out.at[kh - 1], head_in.at[kh - 1], 0, kh, 0))
    for kh, copy in enumerate(back_copies):
        copy.wait_recv()
        both = both + head_in[kh].astype(jnp.float32)
    totals[...] = both.reshape(req_count, ROW_TILE, half)
    last_copies = []
    for kr in range(1, req_count):
        req_out[kr - 1] = totals[req_peer(kr)].astype(jnp.bfloat16)
        last_copies.append(send(req_out.at[kr - 1], req_in.at[kr - 1], kr, 0, 0))
    pick = lax.broadcasted_iota(jnp.int32, (ROW_TILE, batch), 1) == (
        lax.broadcasted_iota(jnp.int32, (ROW_TILE, batch), 0) + h * rows_here
    )
    pick = pick.astype(jnp.float32).astype(jnp.bfloat16)
    stream = jnp.concatenate(
        [
            jnp.dot(pick, hidden[p * head_count + c, r], preferred_element_type=jnp.float32)
            for c in range(head_count)
        ],
        axis=1,
    )
    total = stream + totals[r]
    for kr, copy in enumerate(last_copies):
        copy.wait_recv()
        total = total + req_in[kr].astype(jnp.float32)
    decoded[...] = total[:rows_here].astype(jnp.bfloat16)
    for copy in sent:
        copy.wait_send()


def local(*arguments):
    queries, new_entries, cache_pages, page_table = arguments[:4]
    residual, expert_choice = arguments[7], arguments[10]
    rows_here = residual.shape[0]
    expert_count = lax.axis_size("req") * lax.axis_size("head")
    capacity = max(
        2,
        min(
            rows_here,
            (2 * rows_here * expert_choice.shape[1] + expert_count - 1) // expert_count,
        ),
    )
    fits = (
        capacity == rows_here
        and rows_here <= ROW_TILE
        and expert_count <= 128
        and cache_pages.shape[0] == 1
        and page_table.shape[2] == 1
        and cache_pages.shape[2] == ROW_TILE
        and queries.shape[0] % ROW_TILE == 0
        and queries.shape[0] == rows_here * lax.axis_size("head")
        and lax.axis_size("pool") == 2
        and new_entries.shape[1] == 2
        and arguments[12].shape[0] == 1
    )
    if not fits:
        return local_routed(*arguments)
    return local_dense(*arguments)


def local_dense(
    queries,
    new_entries,
    cache_pages,
    page_table,
    cached_length,
    leave_slots,
    arrive_slots,
    residual,
    norm_gain,
    output_weight,
    expert_choice,
    route_weight,
    gate_up,
    down_weight,
):
    reqs, heads, pools = lax.axis_size("req"), lax.axis_size("head"), lax.axis_size("pool")
    batch = queries.shape[0]
    rows_here, width = residual.shape
    slots, page, entry = cache_pages.shape[1:]
    head_dim = entry // 2
    group_size = queries.shape[1] // head_dim
    moves = leave_slots.shape[0]
    fresh = new_entries.reshape(batch, -1, entry).transpose(1, 0, 2)
    col_block = width // (heads * pools)
    half = width // pools
    chunks = batch // ROW_TILE
    half_rows = group_size // pools * ROW_TILE
    group_rows = reqs * ROW_TILE
    units = gate_up.shape[2]
    copies = (
        1
        + (reqs * heads - 1)
        + 2
        + (heads * pools - 1)
        + (reqs - 1)
        + reqs * (heads - 1)
        + reqs * heads
        + heads
        + (heads - 1)
        + (reqs - 1)
    )
    smem = pl.BlockSpec(memory_space=pltpu.SMEM)
    vmem = pl.BlockSpec(memory_space=pltpu.VMEM)
    hbm = pl.BlockSpec(memory_space=pl.ANY)
    narrow, full = jnp.bfloat16, jnp.float32
    return pl.pallas_call(
        functools.partial(layer_kernel, reqs, heads, pools),
        out_shape=jax.ShapeDtypeStruct((rows_here, half), narrow),
        in_specs=[smem] * 3 + [vmem] * 5 + [hbm] * 6,
        out_specs=vmem,
        scratch_shapes=[
            pltpu.VMEM(queries.shape, narrow),
            pltpu.VMEM(fresh.shape[1:], narrow),
            pltpu.VMEM((slots, page, entry), narrow),
            pltpu.VMEM(output_weight.shape, narrow),
            pltpu.VMEM(gate_up.shape[1:], narrow),
            pltpu.VMEM(down_weight.shape[1:], narrow),
            pltpu.VMEM((moves, page, entry), narrow),
            pltpu.VMEM((moves, page, entry), narrow),
            pltpu.VMEM((batch, page, entry), narrow),
            pltpu.VMEM((heads * reqs, ROW_TILE, 128), full),
            pltpu.VMEM((pools, chunks, half_rows, head_dim), narrow),
            pltpu.VMEM((chunks, half_rows, head_dim), narrow),
            pltpu.VMEM((pools, chunks, half_rows, head_dim), full),
            pltpu.VMEM((chunks, half_rows, head_dim), full),
            pltpu.VMEM((heads * pools, batch, col_block), narrow),
            pltpu.VMEM((heads * pools, batch, col_block), narrow),
            pltpu.VMEM((heads * pools, reqs, batch, col_block), narrow),
            pltpu.VMEM((heads, group_rows, units), narrow),
            pltpu.VMEM((heads, group_rows, half), full),
            pltpu.VMEM((heads, group_rows, half), narrow),
            pltpu.VMEM((heads, group_rows, half), narrow),
            pltpu.VMEM((heads - 1, group_rows, half), narrow),
            pltpu.VMEM((heads - 1, group_rows, half), narrow),
            pltpu.VMEM((reqs, ROW_TILE, half), full),
            pltpu.VMEM((reqs - 1, ROW_TILE, half), narrow),
            pltpu.VMEM((reqs - 1, ROW_TILE, half), narrow),
            pltpu.SemaphoreType.DMA((6,)),
            pltpu.SemaphoreType.DMA((copies,)),
            pltpu.SemaphoreType.DMA((copies,)),
        ],
        compiler_params=pltpu.CompilerParams(
            collective_id=0, has_side_effects=True, vmem_limit_bytes=56 * 1024 * 1024
        ),
        name="layer",
    )(
        page_table.reshape(-1),
        leave_slots,
        arrive_slots,
        cached_length,
        expert_choice,
        route_weight,
        residual,
        norm_gain.reshape(1, -1),
        queries,
        fresh,
        cache_pages,
        output_weight,
        gate_up,
        down_weight,
    )


def solution(mesh):
    return jax.shard_map(
        local,
        mesh=mesh,
        in_specs=(
            P(("group", "req"), "head"),
            P(("group", "req"), None, "head", None),
            P("head", ("group", "req", "pool"), None, None),
            P(("group", "req"), "pool", None),
            P(("group", "req"), "pool"),
            P(("group", "req", "pool")),
            P(("group", "req", "pool")),
            P(("group", "req", "head"), None),
            P(),
            P(("head", "pool"), None),
            P(("group", "req", "head"), None),
            P(("group", "req", "head"), None),
            P(("req", "head"), None, "pool", None),
            P(("req", "head"), "pool", None),
        ),
        out_specs=P(("group", "req", "head"), "pool"),
        check_vma=False,
    )
```

```python
import functools

import jax
import jax.numpy as jnp
from jax import lax
from jax.experimental import pallas as pl
from jax.experimental.pallas import tpu as pltpu
from jax.sharding import PartitionSpec as P

MESH = pl.DeviceIdType.MESH
ROW_TILE = 16
NEGATIVE = -1e30


def swapped(value, axis, apart):
    mask = 2**apart
    pairs = [(source, source ^ mask) for source in range(lax.axis_size(axis))]
    return lax.ppermute(value, axis, pairs)


def combined_all(shard, axis, join):
    gathered = jax.tree.map(
        lambda a, kind: lax.all_gather(a.astype(kind), axis),
        shard,
        (jnp.bfloat16, jnp.bfloat16, jnp.bfloat16),
    )

    def take(source):
        return jax.tree.map(
            lambda a, own: lax.dynamic_index_in_dim(a, source, 0, False).astype(own.dtype),
            gathered,
            shard,
        )

    return lax.fori_loop(
        1, lax.axis_size(axis), lambda source, state: join(state, take(source)), take(0)
    )


def merge_parts(earlier, later):
    first_max, first_denominator, first_value = earlier
    second_max, second_denominator, second_value = later
    largest = jnp.maximum(first_max, second_max)
    first_scale = jnp.exp(first_max - largest)
    second_scale = jnp.exp(second_max - largest)
    denominator = first_denominator * first_scale + second_denominator * second_scale
    weighted = first_value * first_scale[..., None] + second_value * second_scale[..., None]
    return (largest, denominator, weighted)


def local_routed(
    queries,
    new_entries,
    cache_pages,
    page_table,
    cached_length,
    leave_slots,
    arrive_slots,
    residual,
    norm_gain,
    output_weight,
    expert_choice,
    route_weight,
    gate_up,
    down_weight,
):
    batch_size = queries.shape[0]
    group_count = cache_pages.shape[0]
    head_dim = new_entries.shape[3] // 2
    group_size = queries.shape[1] // (group_count * head_dim)
    pool_index = lax.axis_index("pool")
    outgoing = cache_pages[:, leave_slots]
    arrived = swapped(outgoing, "pool", 0)
    current = cache_pages.at[:, arrive_slots].set(arrived)
    context = current[:, page_table[:, 0, :]]
    context = context.reshape(group_count, batch_size, -1, 2 * head_dim)
    context_keys = context[..., :head_dim]
    context_values = context[..., head_dim:]
    grouped_queries = queries.reshape(batch_size, group_count, group_size, head_dim)
    score_scale = head_dim ** (-0.5)
    attention_scores = (
        jnp.einsum(
            "bgqd,gbtd->bgqt", grouped_queries, context_keys, preferred_element_type=jnp.float32
        )
        * score_scale
    )
    positions = jnp.arange(context.shape[2], dtype=jnp.int32)
    valid_mask = positions[None, :] < cached_length
    attention_scores = jnp.where(valid_mask[:, None, None, :], attention_scores, -jnp.inf)
    fresh_scores = (
        jnp.einsum(
            "bgqd,bsgd->bgqs",
            grouped_queries,
            new_entries[..., :head_dim],
            preferred_element_type=jnp.float32,
        )
        * score_scale
    )
    fresh_scores = jnp.where(pool_index == 0, fresh_scores, -jnp.inf)
    largest = jnp.maximum(jnp.max(attention_scores, axis=-1), jnp.max(fresh_scores, axis=-1))
    local_weights = jnp.exp(attention_scores - largest[..., None])
    fresh_weights = jnp.exp(fresh_scores - largest[..., None])
    denominator = jnp.sum(local_weights, axis=-1) + jnp.sum(fresh_weights, axis=-1)
    weighted = jnp.einsum("bgqt,gbtd->bgqd", local_weights, context_values.astype(jnp.float32))
    weighted = weighted + jnp.einsum(
        "bgqs,bsgd->bgqd", fresh_weights, new_entries[..., head_dim:].astype(jnp.float32)
    )
    largest, denominator, weighted = combined_all(
        (largest, denominator, weighted), "pool", merge_parts
    )
    attended = (weighted / denominator[..., None]).reshape(batch_size, -1).astype(jnp.bfloat16)
    head_width = output_weight.shape[0]
    own_heads = lax.dynamic_slice_in_dim(attended, pool_index * head_width, head_width, 1)
    partial_value = jnp.dot(own_heads, output_weight, preferred_element_type=jnp.float32)
    rows_here = residual.shape[0]
    summed = lax.psum(partial_value.astype(jnp.bfloat16), ("head", "pool")).astype(jnp.float32)
    attention = lax.dynamic_slice_in_dim(summed, lax.axis_index("head") * rows_here, rows_here, 0)
    hidden = residual.astype(jnp.float32) + attention
    normed = (
        hidden * lax.rsqrt(jnp.mean(hidden * hidden, axis=-1, keepdims=True) + 1e-06) * norm_gain
    ).astype(jnp.bfloat16)
    expert_count = lax.axis_size("req") * lax.axis_size("head")
    top_count = expert_choice.shape[1]
    capacity = max(
        2, min(rows_here, (2 * rows_here * top_count + expert_count - 1) // expert_count)
    )
    flat_choice = expert_choice.reshape(-1)
    expert_hits = (
        flat_choice[:, None] == jnp.arange(expert_count, dtype=jnp.int32)[None, :]
    ).astype(jnp.int32)
    earlier = jnp.cumsum(expert_hits, axis=0) - expert_hits
    slot_index = jnp.sum(earlier * expert_hits, axis=1)
    target = flat_choice * capacity + slot_index
    placed = (
        target[:, None] == jnp.arange(expert_count * capacity, dtype=jnp.int32)[None, :]
    ).astype(jnp.float32)
    placed = placed.reshape(rows_here, top_count, expert_count * capacity)
    dispatch = jnp.sum(placed, axis=1).astype(jnp.bfloat16)
    combine_matrix = jnp.sum(placed * route_weight[:, :, None], axis=1)
    outgoing_rows = jnp.einsum("re,rd->ed", dispatch, normed, preferred_element_type=jnp.float32)
    outgoing_rows = outgoing_rows.astype(jnp.bfloat16).reshape(expert_count, capacity, -1)
    model_width = normed.shape[1]
    half_width = model_width // lax.axis_size("pool")
    projection = gate_up[0].reshape(-1, model_width)
    hidden_size = projection.shape[0] // 2
    received = lax.all_to_all(
        outgoing_rows, ("req", "head"), split_axis=0, concat_axis=0, tiled=True
    )
    sources = received.shape[0]
    item_count = received.shape[1]
    flat_rows = received.reshape(sources * item_count, model_width)
    projected = jnp.einsum("nd,fd->nf", flat_rows, projection, preferred_element_type=jnp.float32)
    activated = (jax.nn.silu(projected[:, :hidden_size]) * projected[:, hidden_size:]).astype(
        jnp.bfloat16
    )
    part_sum = jnp.dot(activated, down_weight[0], preferred_element_type=jnp.float32).reshape(
        sources, item_count, model_width
    )
    column_sum = lax.psum_scatter(
        part_sum.astype(jnp.bfloat16), "pool", scatter_dimension=2, tiled=True
    )
    returned = lax.all_to_all(column_sum, ("req", "head"), split_axis=0, concat_axis=0, tiled=True)
    gathered = returned.reshape(expert_count * capacity, half_width).astype(jnp.float32)
    expert_mix = jnp.dot(combine_matrix, gathered, precision=lax.Precision.HIGHEST)
    own_columns = lax.dynamic_slice_in_dim(hidden, pool_index * half_width, half_width, 1)
    return (own_columns + expert_mix).astype(jnp.bfloat16)


def layer_kernel(
    req_count,
    head_count,
    pool_count,
    page_table,
    leave_slots,
    arrive_slots,
    cached_length,
    expert_choice,
    route_weight,
    residual,
    norm_gain,
    queries_hbm,
    fresh_hbm,
    cache_hbm,
    output_weight_hbm,
    gate_up_hbm,
    down_weight_hbm,
    decoded,
    queries,
    fresh,
    cache,
    output_weight,
    gate_up,
    down_weight,
    leaving,
    arrived,
    context,
    weights,
    values_out,
    values_in,
    level_out,
    level_in,
    partial_out,
    partial_in,
    hidden,
    active,
    own_part,
    pool_out,
    pool_in,
    head_out,
    head_in,
    totals,
    req_out,
    req_in,
    load_sem,
    send_sem,
    recv_sem,
):
    r, h, p = lax.axis_index("req"), lax.axis_index("head"), lax.axis_index("pool")
    batch, page = queries.shape[0], cache.shape[1]
    head_dim = cache.shape[2] // 2
    group_size = queries.shape[1] // head_dim
    rows_here = residual.shape[0]
    width = residual.shape[1]
    col_block = width // (head_count * pool_count)
    half = width // pool_count
    half_heads = group_size // pool_count
    chunks = batch // ROW_TILE
    moves = leaving.shape[0]

    loads = [
        pltpu.make_async_copy(source, target, load_sem.at[i])
        for i, (source, target) in enumerate(
            (
                (cache_hbm.at[0], cache),
                (queries_hbm, queries),
                (fresh_hbm, fresh),
                (output_weight_hbm, output_weight),
                (gate_up_hbm.at[0], gate_up),
                (down_weight_hbm.at[0], down_weight),
            )
        )
    ]
    for load in loads:
        load.start()

    def req_peer(k):
        return lax.rem(r + k, req_count)

    def head_peer(k):
        return lax.rem(h + k, head_count)

    def req_source(k):
        return lax.rem(r + req_count - k, req_count)

    def head_source(k):
        return lax.rem(h + head_count - k, head_count)

    partner = 1 - p
    barrier = pltpu.get_barrier_semaphore()
    peers = [
        (kr, kh, kp)
        for kr in range(req_count)
        for kh in range(head_count)
        for kp in range(pool_count)
        if (kr, kh, kp) != (0, 0, 0) and (kp == 0 or kr == 0)
    ]

    def where_is(kr, kh, kp):
        return {
            "req": req_peer(kr) if kr else r,
            "head": head_peer(kh) if kh else h,
            "pool": partner if kp else p,
        }

    for peer in peers:
        pl.semaphore_signal(barrier, inc=1, device_id=where_is(*peer), device_id_type=MESH)

    experts = weights.shape[1]
    named = lax.broadcasted_iota(jnp.int32, (experts, rows_here), 0)
    dense = jnp.zeros((experts, rows_here), jnp.float32)
    for k in range(expert_choice.shape[0]):
        dense = dense + jnp.where(named == expert_choice[k : k + 1, :], route_weight[k : k + 1, :], 0.0)
    own_block = h * req_count + r
    weights[own_block] = jnp.concatenate(
        [dense, jnp.zeros((experts, weights.shape[2] - rows_here), jnp.float32)], axis=1
    )

    sent = []

    def send(source, target, kr, kh, kp):
        at = len(sent)
        copy = pltpu.make_async_remote_copy(
            src_ref=source,
            dst_ref=target,
            send_sem=send_sem.at[at],
            recv_sem=recv_sem.at[at],
            device_id=where_is(kr, kh, kp),
            device_id_type=MESH,
        )
        copy.start()
        sent.append(copy)
        return copy

    loads[0].wait()
    for k in range(moves):
        leaving[k] = cache[leave_slots[k]]
    pl.semaphore_wait(barrier, len(peers))
    pages = send(leaving, arrived, 0, 0, 1)
    weight_copies = [
        send(weights.at[own_block], weights.at[own_block], kr, kh, 0)
        for kr in range(req_count)
        for kh in range(head_count)
        if kr or kh
    ]
    loads[1].wait()
    loads[2].wait()
    pages.wait_recv()

    def gather(b, carry):
        slot = page_table[b]
        which, moved = jnp.int32(0), jnp.int32(0)
        for k in range(moves):
            hit = arrive_slots[k] == slot
            which = jnp.where(hit, k, which)
            moved = jnp.where(hit, 1, moved)
        flag = jnp.full((page, 2 * head_dim), moved, jnp.int32) > 0
        kept = cache[slot].astype(jnp.float32)
        swapped_in = arrived[which].astype(jnp.float32)
        context[b] = jnp.where(flag, swapped_in, kept).astype(jnp.bfloat16)
        return carry

    lax.fori_loop(0, batch, gather, 0, unroll=8)

    tile_rows = group_size * ROW_TILE
    here = lax.broadcasted_iota(jnp.int32, (batch, batch), 0)
    there = lax.broadcasted_iota(jnp.int32, (batch, batch), 1)
    lengths = jnp.where(here == there, cached_length[...].astype(jnp.float32), 0.0)
    lengths = jnp.sum(lengths, axis=-1, keepdims=True)
    to_entry = lax.broadcasted_iota(jnp.int32, (ROW_TILE, 2 * ROW_TILE), 1) == (
        2 * lax.broadcasted_iota(jnp.int32, (ROW_TILE, 2 * ROW_TILE), 0) + p
    )
    to_entry = to_entry.astype(jnp.float32).astype(jnp.bfloat16)
    to_entry = jnp.concatenate([to_entry] * group_size, axis=0)
    score_scale = head_dim ** (-0.5)
    for c in range(chunks):
        base = c * ROW_TILE
        stacked = jnp.concatenate(
            [
                queries[base : base + ROW_TILE, g * head_dim : (g + 1) * head_dim]
                for g in range(group_size)
            ],
            axis=0,
        )
        block = context[base : base + ROW_TILE].reshape(ROW_TILE * page, 2 * head_dim)
        scores = (
            lax.dot_general(
                stacked,
                block[:, :head_dim],
                (((1,), (1,)), ((), ())),
                preferred_element_type=jnp.float32,
            )
            * score_scale
        )
        shape = (ROW_TILE, ROW_TILE * page)
        first = lax.broadcasted_iota(jnp.int32, shape, 0) * page
        offset = lax.broadcasted_iota(jnp.int32, shape, 1) - first
        live = (offset >= 0) & (
            offset.astype(jnp.float32) < lengths[base : base + ROW_TILE]
        )
        bias = jnp.where(live, 0.0, NEGATIVE)
        bias = jnp.concatenate([bias] * group_size, axis=0)
        scores = jnp.where(bias < 0.0, NEGATIVE, scores)
        newest = fresh[base : base + ROW_TILE].reshape(2 * ROW_TILE, 2 * head_dim)
        newest = jnp.dot(to_entry, newest, preferred_element_type=jnp.float32)
        fresh_score = (
            jnp.sum(stacked.astype(jnp.float32) * newest[:, :head_dim], axis=-1, keepdims=True)
            * score_scale
        )
        largest = jnp.maximum(jnp.max(scores, axis=-1, keepdims=True), fresh_score)
        raised = jnp.exp(scores - largest)
        fresh_raised = jnp.exp(fresh_score - largest)
        denominator = jnp.sum(raised, axis=-1, keepdims=True) + fresh_raised
        value = jnp.dot(
            raised.astype(jnp.bfloat16), block[:, head_dim:], preferred_element_type=jnp.float32
        )
        value = (value + fresh_raised * newest[:, head_dim:]) / denominator
        level = jnp.broadcast_to(largest + jnp.log(denominator), (tile_rows, head_dim))
        for s in range(pool_count):
            rows = slice(s * half_heads * ROW_TILE, (s + 1) * half_heads * ROW_TILE)
            values_out[s, c] = value[rows].astype(jnp.bfloat16)
            level_out[s, c] = level[rows]
    value_copy = send(values_out.at[partner], values_in, 0, 0, 1)
    level_copy = send(level_out.at[partner], level_in, 0, 0, 1)

    spread = lax.broadcasted_iota(jnp.int32, (batch, rows_here), 0) == (
        lax.broadcasted_iota(jnp.int32, (batch, rows_here), 1) + h * rows_here
    )
    spread = jnp.where(p == 0, spread.astype(jnp.float32), 0.0).astype(jnp.bfloat16)
    loads[3].wait()
    value_copy.wait_recv()
    level_copy.wait_recv()
    merged = []
    for c in range(chunks):
        first_level, second_level = level_out[p, c], level_in[c]
        top = jnp.maximum(first_level, second_level)
        first_share = jnp.exp(first_level - top)
        second_share = jnp.exp(second_level - top)
        value = values_out[p, c].astype(jnp.float32) * first_share
        value = value + values_in[c].astype(jnp.float32) * second_share
        value = (value / (first_share + second_share)).astype(jnp.bfloat16)
        merged.append(
            jnp.concatenate(
                [value[g * ROW_TILE : (g + 1) * ROW_TILE] for g in range(half_heads)], axis=1
            )
        )
    merged = jnp.concatenate(merged, axis=0)
    blocks = head_count * pool_count
    for d in range(blocks):
        columns = slice(d * col_block, (d + 1) * col_block)
        part = jnp.dot(merged, output_weight[:, columns], preferred_element_type=jnp.float32)
        part = part + jnp.dot(spread, residual[:, columns], preferred_element_type=jnp.float32)
        partial_out[d] = part.astype(jnp.bfloat16)
    partial_copies = []
    for kh in list(range(1, head_count)) + [0]:
        for kp in range(pool_count):
            if kh or kp:
                to_pool = partner if kp else p
                to_head = head_peer(kh) if kh else h
                partial_copies.append(
                    send(
                        partial_out.at[to_pool * head_count + to_head],
                        partial_in.at[kh * pool_count + kp],
                        0,
                        kh,
                        kp,
                    )
                )
    mine = p * head_count + h
    summed = partial_out[mine].astype(jnp.float32)
    order = [kh * pool_count + kp for kh in list(range(1, head_count)) + [0] for kp in range(pool_count) if kh or kp]
    for copy, slot in zip(partial_copies, order):
        copy.wait_recv()
        summed = summed + partial_in[slot].astype(jnp.float32)
    hidden[mine, r] = summed.astype(jnp.bfloat16)

    def hidden_block(at_head, at_req):
        return hidden.at[p * head_count + at_head, at_req]

    own_hidden = hidden_block(h, r)
    req_copies = {kr: send(own_hidden, own_hidden, kr, 0, 0) for kr in range(1, req_count)}
    head_copies, pool_copies = {}, {}
    for kh in range(1, head_count):
        head_copies[kh, 0] = send(own_hidden, own_hidden, 0, kh, 0)
    pool_copies[0, 0] = send(own_hidden, own_hidden, 0, 0, 1)
    for kr in range(1, req_count):
        req_copies[kr].wait_recv()
        block = hidden_block(h, req_source(kr))
        for kh in range(1, head_count):
            head_copies[kh, kr] = send(block, block, 0, kh, 0)
        pool_copies[0, kr] = send(block, block, 0, 0, 1)

    loads[4].wait()
    row_count = req_count * batch
    units = gate_up.shape[1]
    gate = jnp.zeros((row_count, units), jnp.float32)
    up = jnp.zeros((row_count, units), jnp.float32)
    squares = jnp.zeros((row_count, 1), jnp.float32)

    def accumulate(state, chunk):
        gate, up, squares = state
        x = hidden[chunk].reshape(row_count, col_block).astype(jnp.float32)
        columns = pl.ds(pl.multiple_of(chunk * col_block, col_block), col_block)
        scaled = (x * norm_gain[:, columns]).astype(jnp.bfloat16)
        contract = (((1,), (1,)), ((), ()))
        gate = gate + lax.dot_general(
            scaled, gate_up[0, :, columns], contract, preferred_element_type=jnp.float32
        )
        up = up + lax.dot_general(
            scaled, gate_up[1, :, columns], contract, preferred_element_type=jnp.float32
        )
        return gate, up, squares + jnp.sum(x * x, axis=-1, keepdims=True)

    state = (gate, up, squares)
    state = accumulate(state, mine)
    for kh in range(1, head_count):
        for kr in range(req_count):
            head_copies[kh, kr].wait_recv()
            block = hidden_block(head_source(kh), req_source(kr) if kr else r)
            pool_copies[kh, kr] = send(block, block, 0, 0, 1)
        state = accumulate(state, p * head_count + head_source(kh))
    for kh in range(head_count):
        for kr in range(req_count):
            pool_copies[kh, kr].wait_recv()
        state = accumulate(state, partner * head_count + (head_source(kh) if kh else h))
    gate, up, squares = state
    scale = lax.rsqrt(squares * (1.0 / width) + 1e-06)
    gate = gate * scale
    activated = (gate / (1.0 + jnp.exp(-gate)) * (up * scale)).astype(jnp.bfloat16)
    place_row = lax.broadcasted_iota(jnp.int32, (ROW_TILE, row_count), 0)
    place_col = lax.broadcasted_iota(jnp.int32, (ROW_TILE, row_count), 1)
    for copy in weight_copies:
        copy.wait_recv()
    for to_head in range(head_count):
        placing = jnp.concatenate(
            [
                (
                    (place_row + (to_req * batch + to_head * rows_here) == place_col)
                    & (place_row < rows_here)
                )
                .astype(jnp.float32)
                .astype(jnp.bfloat16)
                for to_req in range(req_count)
            ],
            axis=0,
        )
        active[to_head] = jnp.dot(placing, activated, preferred_element_type=jnp.float32).astype(
            jnp.bfloat16
        )
    loads[5].wait()
    expert = r * head_count + h
    diagonal = lax.broadcasted_iota(jnp.int32, (ROW_TILE, weights.shape[2]), 0) == (
        lax.broadcasted_iota(jnp.int32, (ROW_TILE, weights.shape[2]), 1)
    )

    def expert_part(to_head, side):
        weight = jnp.concatenate(
            [
                jnp.where(diagonal, weights[to_head * req_count + k, pl.ds(expert, 1), :], 0.0)
                for k in range(req_count)
            ],
            axis=0,
        )
        weight = jnp.sum(weight, axis=-1, keepdims=True)
        columns = pl.ds(pl.multiple_of(side * half, half), half)
        value = jnp.dot(
            active[to_head], down_weight[:, columns], preferred_element_type=jnp.float32
        )
        return value * weight

    turn = list(range(1, head_count)) + [0]
    swap_copies = {}
    for kh in turn:
        pool_out[kh] = expert_part(head_peer(kh) if kh else h, partner).astype(jnp.bfloat16)
        swap_copies[kh] = send(pool_out.at[kh], pool_in.at[kh], 0, 0, 1)
    for kh in turn:
        own_part[kh] = expert_part(head_peer(kh) if kh else h, p)
    back_copies = []
    for kh in turn:
        swap_copies[kh].wait_recv()
        both = own_part[kh] + pool_in[kh].astype(jnp.float32)
        if kh:
            head_out[kh - 1] = both.reshape(req_count, ROW_TILE, half)[:, :rows_here].astype(jnp.bfloat16)
            back_copies.append(send(head_out.at[kh - 1], head_in.at[kh - 1], 0, kh, 0))
    both = both.reshape(req_count, ROW_TILE, half)[:, :rows_here]
    for kh, copy in enumerate(back_copies):
        copy.wait_recv()
        both = both + head_in[kh].astype(jnp.float32)
    totals[...] = both
    last_copies = []
    for kr in range(1, req_count):
        req_out[kr - 1] = totals[req_peer(kr)].astype(jnp.bfloat16)
        last_copies.append(send(req_out.at[kr - 1], req_in.at[kr - 1], kr, 0, 0))
    pick = lax.broadcasted_iota(jnp.int32, (ROW_TILE, batch), 1) == (
        lax.broadcasted_iota(jnp.int32, (ROW_TILE, batch), 0) + h * rows_here
    )
    pick = pick.astype(jnp.float32).astype(jnp.bfloat16)
    stream = jnp.concatenate(
        [
            jnp.dot(pick, hidden[p * head_count + c, r], preferred_element_type=jnp.float32)
            for c in range(head_count)
        ],
        axis=1,
    )
    total = stream[:rows_here] + totals[r]
    for kr, copy in enumerate(last_copies):
        copy.wait_recv()
        total = total + req_in[kr].astype(jnp.float32)
    decoded[...] = total.astype(jnp.bfloat16)
    for copy in sent:
        copy.wait_send()


def local(*arguments):
    queries, new_entries, cache_pages, page_table = arguments[:4]
    residual, expert_choice = arguments[7], arguments[10]
    rows_here = residual.shape[0]
    expert_count = lax.axis_size("req") * lax.axis_size("head")
    capacity = max(
        2,
        min(
            rows_here,
            (2 * rows_here * expert_choice.shape[1] + expert_count - 1) // expert_count,
        ),
    )
    fits = (
        capacity == rows_here
        and rows_here <= ROW_TILE
        and expert_count <= 128
        and cache_pages.shape[0] == 1
        and page_table.shape[2] == 1
        and cache_pages.shape[2] == ROW_TILE
        and queries.shape[0] % ROW_TILE == 0
        and queries.shape[0] == rows_here * lax.axis_size("head")
        and lax.axis_size("pool") == 2
        and new_entries.shape[1] == 2
        and arguments[12].shape[0] == 1
    )
    if not fits:
        return local_routed(*arguments)
    return local_dense(*arguments)


def local_dense(
    queries,
    new_entries,
    cache_pages,
    page_table,
    cached_length,
    leave_slots,
    arrive_slots,
    residual,
    norm_gain,
    output_weight,
    expert_choice,
    route_weight,
    gate_up,
    down_weight,
):
    reqs, heads, pools = lax.axis_size("req"), lax.axis_size("head"), lax.axis_size("pool")
    batch = queries.shape[0]
    rows_here, width = residual.shape
    slots, page, entry = cache_pages.shape[1:]
    head_dim = entry // 2
    group_size = queries.shape[1] // head_dim
    moves = leave_slots.shape[0]
    fresh = new_entries.reshape(batch, -1, entry)
    col_block = width // (heads * pools)
    half = width // pools
    chunks = batch // ROW_TILE
    half_rows = group_size // pools * ROW_TILE
    group_rows = reqs * ROW_TILE
    units = gate_up.shape[2]
    copies = (
        1
        + (reqs * heads - 1)
        + 2
        + (heads * pools - 1)
        + (reqs - 1)
        + reqs * (heads - 1)
        + reqs * heads
        + heads
        + (heads - 1)
        + (reqs - 1)
    )
    smem = pl.BlockSpec(memory_space=pltpu.SMEM)
    vmem = pl.BlockSpec(memory_space=pltpu.VMEM)
    hbm = pl.BlockSpec(memory_space=pl.ANY)
    narrow, full = jnp.bfloat16, jnp.float32
    return pl.pallas_call(
        functools.partial(layer_kernel, reqs, heads, pools),
        out_shape=jax.ShapeDtypeStruct((rows_here, half), narrow),
        in_specs=[smem] * 3 + [vmem] * 5 + [hbm] * 6,
        out_specs=vmem,
        scratch_shapes=[
            pltpu.VMEM(queries.shape, narrow),
            pltpu.VMEM(fresh.shape, narrow),
            pltpu.VMEM((slots, page, entry), narrow),
            pltpu.VMEM(output_weight.shape, narrow),
            pltpu.VMEM(gate_up.shape[1:], narrow),
            pltpu.VMEM(down_weight.shape[1:], narrow),
            pltpu.VMEM((moves, page, entry), narrow),
            pltpu.VMEM((moves, page, entry), narrow),
            pltpu.VMEM((batch, page, entry), narrow),
            pltpu.VMEM((heads * reqs, -(-reqs * heads // 8) * 8, 128), full),
            pltpu.VMEM((pools, chunks, half_rows, head_dim), narrow),
            pltpu.VMEM((chunks, half_rows, head_dim), narrow),
            pltpu.VMEM((pools, chunks, half_rows, head_dim), full),
            pltpu.VMEM((chunks, half_rows, head_dim), full),
            pltpu.VMEM((heads * pools, batch, col_block), narrow),
            pltpu.VMEM((heads * pools, batch, col_block), narrow),
            pltpu.VMEM((heads * pools, reqs, batch, col_block), narrow),
            pltpu.VMEM((heads, group_rows, units), narrow),
            pltpu.VMEM((heads, group_rows, half), full),
            pltpu.VMEM((heads, group_rows, half), narrow),
            pltpu.VMEM((heads, group_rows, half), narrow),
            pltpu.VMEM((heads - 1, reqs, rows_here, half), narrow),
            pltpu.VMEM((heads - 1, reqs, rows_here, half), narrow),
            pltpu.VMEM((reqs, rows_here, half), full),
            pltpu.VMEM((reqs - 1, rows_here, half), narrow),
            pltpu.VMEM((reqs - 1, rows_here, half), narrow),
            pltpu.SemaphoreType.DMA((6,)),
            pltpu.SemaphoreType.DMA((copies,)),
            pltpu.SemaphoreType.DMA((copies,)),
        ],
        compiler_params=pltpu.CompilerParams(
            collective_id=0, has_side_effects=True, vmem_limit_bytes=56 * 1024 * 1024
        ),
        name="layer",
    )(
        page_table.reshape(-1),
        leave_slots,
        arrive_slots,
        cached_length.T,
        expert_choice.T,
        route_weight.T,
        residual,
        norm_gain.reshape(1, -1),
        queries,
        fresh,
        cache_pages,
        output_weight,
        gate_up,
        down_weight,
    )


def solution(mesh):
    return jax.shard_map(
        local,
        mesh=mesh,
        in_specs=(
            P(("group", "req"), "head"),
            P(("group", "req"), None, "head", None),
            P("head", ("group", "req", "pool"), None, None),
            P(("group", "req"), "pool", None),
            P(("group", "req"), "pool"),
            P(("group", "req", "pool")),
            P(("group", "req", "pool")),
            P(("group", "req", "head"), None),
            P(),
            P(("head", "pool"), None),
            P(("group", "req", "head"), None),
            P(("group", "req", "head"), None),
            P(("req", "head"), None, "pool", None),
            P(("req", "head"), "pool", None),
        ),
        out_specs=P(("group", "req", "head"), "pool"),
        check_vma=False,
    )
```

```python
import functools

import jax
import jax.numpy as jnp
from jax import lax
from jax.experimental import pallas as pl
from jax.experimental.pallas import tpu as pltpu
from jax.sharding import PartitionSpec as P

MESH = pl.DeviceIdType.MESH
ROW_TILE = 16
NEGATIVE = -1e30


def swapped(value, axis, apart):
    mask = 2**apart
    pairs = [(source, source ^ mask) for source in range(lax.axis_size(axis))]
    return lax.ppermute(value, axis, pairs)


def combined_all(shard, axis, join):
    gathered = jax.tree.map(
        lambda a, kind: lax.all_gather(a.astype(kind), axis),
        shard,
        (jnp.bfloat16, jnp.bfloat16, jnp.bfloat16),
    )

    def take(source):
        return jax.tree.map(
            lambda a, own: lax.dynamic_index_in_dim(a, source, 0, False).astype(own.dtype),
            gathered,
            shard,
        )

    return lax.fori_loop(
        1, lax.axis_size(axis), lambda source, state: join(state, take(source)), take(0)
    )


def merge_parts(earlier, later):
    first_max, first_denominator, first_value = earlier
    second_max, second_denominator, second_value = later
    largest = jnp.maximum(first_max, second_max)
    first_scale = jnp.exp(first_max - largest)
    second_scale = jnp.exp(second_max - largest)
    denominator = first_denominator * first_scale + second_denominator * second_scale
    weighted = first_value * first_scale[..., None] + second_value * second_scale[..., None]
    return (largest, denominator, weighted)


def local_routed(
    queries,
    new_entries,
    cache_pages,
    page_table,
    cached_length,
    leave_slots,
    arrive_slots,
    residual,
    norm_gain,
    output_weight,
    expert_choice,
    route_weight,
    gate_up,
    down_weight,
):
    batch_size = queries.shape[0]
    group_count = cache_pages.shape[0]
    head_dim = new_entries.shape[3] // 2
    group_size = queries.shape[1] // (group_count * head_dim)
    pool_index = lax.axis_index("pool")
    outgoing = cache_pages[:, leave_slots]
    arrived = swapped(outgoing, "pool", 0)
    current = cache_pages.at[:, arrive_slots].set(arrived)
    context = current[:, page_table[:, 0, :]]
    context = context.reshape(group_count, batch_size, -1, 2 * head_dim)
    context_keys = context[..., :head_dim]
    context_values = context[..., head_dim:]
    grouped_queries = queries.reshape(batch_size, group_count, group_size, head_dim)
    score_scale = head_dim ** (-0.5)
    attention_scores = (
        jnp.einsum(
            "bgqd,gbtd->bgqt", grouped_queries, context_keys, preferred_element_type=jnp.float32
        )
        * score_scale
    )
    positions = jnp.arange(context.shape[2], dtype=jnp.int32)
    valid_mask = positions[None, :] < cached_length
    attention_scores = jnp.where(valid_mask[:, None, None, :], attention_scores, -jnp.inf)
    fresh_scores = (
        jnp.einsum(
            "bgqd,bsgd->bgqs",
            grouped_queries,
            new_entries[..., :head_dim],
            preferred_element_type=jnp.float32,
        )
        * score_scale
    )
    fresh_scores = jnp.where(pool_index == 0, fresh_scores, -jnp.inf)
    largest = jnp.maximum(jnp.max(attention_scores, axis=-1), jnp.max(fresh_scores, axis=-1))
    local_weights = jnp.exp(attention_scores - largest[..., None])
    fresh_weights = jnp.exp(fresh_scores - largest[..., None])
    denominator = jnp.sum(local_weights, axis=-1) + jnp.sum(fresh_weights, axis=-1)
    weighted = jnp.einsum("bgqt,gbtd->bgqd", local_weights, context_values.astype(jnp.float32))
    weighted = weighted + jnp.einsum(
        "bgqs,bsgd->bgqd", fresh_weights, new_entries[..., head_dim:].astype(jnp.float32)
    )
    largest, denominator, weighted = combined_all(
        (largest, denominator, weighted), "pool", merge_parts
    )
    attended = (weighted / denominator[..., None]).reshape(batch_size, -1).astype(jnp.bfloat16)
    head_width = output_weight.shape[0]
    own_heads = lax.dynamic_slice_in_dim(attended, pool_index * head_width, head_width, 1)
    partial_value = jnp.dot(own_heads, output_weight, preferred_element_type=jnp.float32)
    rows_here = residual.shape[0]
    summed = lax.psum(partial_value.astype(jnp.bfloat16), ("head", "pool")).astype(jnp.float32)
    attention = lax.dynamic_slice_in_dim(summed, lax.axis_index("head") * rows_here, rows_here, 0)
    hidden = residual.astype(jnp.float32) + attention
    normed = (
        hidden * lax.rsqrt(jnp.mean(hidden * hidden, axis=-1, keepdims=True) + 1e-06) * norm_gain
    ).astype(jnp.bfloat16)
    expert_count = lax.axis_size("req") * lax.axis_size("head")
    top_count = expert_choice.shape[1]
    capacity = max(
        2, min(rows_here, (2 * rows_here * top_count + expert_count - 1) // expert_count)
    )
    flat_choice = expert_choice.reshape(-1)
    expert_hits = (
        flat_choice[:, None] == jnp.arange(expert_count, dtype=jnp.int32)[None, :]
    ).astype(jnp.int32)
    earlier = jnp.cumsum(expert_hits, axis=0) - expert_hits
    slot_index = jnp.sum(earlier * expert_hits, axis=1)
    target = flat_choice * capacity + slot_index
    placed = (
        target[:, None] == jnp.arange(expert_count * capacity, dtype=jnp.int32)[None, :]
    ).astype(jnp.float32)
    placed = placed.reshape(rows_here, top_count, expert_count * capacity)
    dispatch = jnp.sum(placed, axis=1).astype(jnp.bfloat16)
    combine_matrix = jnp.sum(placed * route_weight[:, :, None], axis=1)
    outgoing_rows = jnp.einsum("re,rd->ed", dispatch, normed, preferred_element_type=jnp.float32)
    outgoing_rows = outgoing_rows.astype(jnp.bfloat16).reshape(expert_count, capacity, -1)
    model_width = normed.shape[1]
    half_width = model_width // lax.axis_size("pool")
    projection = gate_up[0].reshape(-1, model_width)
    hidden_size = projection.shape[0] // 2
    received = lax.all_to_all(
        outgoing_rows, ("req", "head"), split_axis=0, concat_axis=0, tiled=True
    )
    sources = received.shape[0]
    item_count = received.shape[1]
    flat_rows = received.reshape(sources * item_count, model_width)
    projected = jnp.einsum("nd,fd->nf", flat_rows, projection, preferred_element_type=jnp.float32)
    activated = (jax.nn.silu(projected[:, :hidden_size]) * projected[:, hidden_size:]).astype(
        jnp.bfloat16
    )
    part_sum = jnp.dot(activated, down_weight[0], preferred_element_type=jnp.float32).reshape(
        sources, item_count, model_width
    )
    column_sum = lax.psum_scatter(
        part_sum.astype(jnp.bfloat16), "pool", scatter_dimension=2, tiled=True
    )
    returned = lax.all_to_all(column_sum, ("req", "head"), split_axis=0, concat_axis=0, tiled=True)
    gathered = returned.reshape(expert_count * capacity, half_width).astype(jnp.float32)
    expert_mix = jnp.dot(combine_matrix, gathered, precision=lax.Precision.HIGHEST)
    own_columns = lax.dynamic_slice_in_dim(hidden, pool_index * half_width, half_width, 1)
    return (own_columns + expert_mix).astype(jnp.bfloat16)


def layer_kernel(
    req_count,
    head_count,
    pool_count,
    page_table,
    leave_slots,
    arrive_slots,
    cached_length,
    expert_choice,
    route_weight,
    residual,
    norm_gain,
    queries_hbm,
    fresh_hbm,
    cache_hbm,
    output_weight_hbm,
    gate_up_hbm,
    down_weight_hbm,
    decoded,
    queries,
    fresh,
    cache,
    output_weight,
    gate_up,
    down_weight,
    leaving,
    arrived,
    context,
    weights,
    values_out,
    values_in,
    level_out,
    level_in,
    partial_out,
    partial_in,
    hidden,
    active,
    own_part,
    pool_out,
    pool_in,
    head_out,
    head_in,
    totals,
    req_out,
    req_in,
    load_sem,
    send_sem,
    recv_sem,
):
    r, h, p = lax.axis_index("req"), lax.axis_index("head"), lax.axis_index("pool")
    batch, page = queries.shape[0], cache.shape[1]
    head_dim = cache.shape[2] // 2
    group_size = queries.shape[1] // head_dim
    rows_here = residual.shape[0]
    width = residual.shape[1]
    col_block = width // (head_count * pool_count)
    half = width // pool_count
    half_heads = group_size // pool_count
    chunks = batch // ROW_TILE
    moves = leaving.shape[0]

    loads = [
        pltpu.make_async_copy(source, target, load_sem.at[i])
        for i, (source, target) in enumerate(
            (
                (cache_hbm.at[0], cache),
                (queries_hbm, queries),
                (fresh_hbm, fresh),
                (output_weight_hbm, output_weight),
                (gate_up_hbm.at[0], gate_up),
                (down_weight_hbm.at[0], down_weight),
            )
        )
    ]
    for load in loads:
        load.start()

    def req_peer(k):
        return lax.rem(r + k, req_count)

    def head_peer(k):
        return lax.rem(h + k, head_count)

    def req_source(k):
        return lax.rem(r + req_count - k, req_count)

    def head_source(k):
        return lax.rem(h + head_count - k, head_count)

    partner = 1 - p
    barrier = pltpu.get_barrier_semaphore()
    peers = [
        (kr, kh, kp)
        for kr in range(req_count)
        for kh in range(head_count)
        for kp in range(pool_count)
        if (kr, kh, kp) != (0, 0, 0) and (kr > 0) + (kh > 0) + (kp > 0) == 1
    ]

    def where_is(kr, kh, kp):
        return {
            "req": req_peer(kr) if kr else r,
            "head": head_peer(kh) if kh else h,
            "pool": partner if kp else p,
        }

    for peer in peers:
        pl.semaphore_signal(barrier, inc=1, device_id=where_is(*peer), device_id_type=MESH)

    experts = weights.shape[1]
    named = lax.broadcasted_iota(jnp.int32, (experts, rows_here), 0)
    dense = jnp.zeros((experts, rows_here), jnp.float32)
    for k in range(expert_choice.shape[0]):
        dense = dense + jnp.where(named == expert_choice[k : k + 1, :], route_weight[k : k + 1, :], 0.0)
    own_block = h * req_count + r
    weights[own_block] = jnp.concatenate(
        [dense, jnp.zeros((experts, weights.shape[2] - rows_here), jnp.float32)], axis=1
    )

    sent = []

    def send(source, target, kr, kh, kp):
        at = len(sent)
        copy = pltpu.make_async_remote_copy(
            src_ref=source,
            dst_ref=target,
            send_sem=send_sem.at[at],
            recv_sem=recv_sem.at[at],
            device_id=where_is(kr, kh, kp),
            device_id_type=MESH,
        )
        copy.start()
        sent.append(copy)
        return copy

    loads[0].wait()
    for k in range(moves):
        leaving[k] = cache[leave_slots[k]]
    pl.semaphore_wait(barrier, len(peers))
    pages = send(leaving, arrived, 0, 0, 1)
    weight_copies = [
        send(weights.at[own_block], weights.at[own_block], kr, 0, 0) for kr in range(1, req_count)
    ]
    loads[1].wait()
    loads[2].wait()
    pages.wait_recv()

    def gather(b, carry):
        slot = page_table[b]
        which, moved = jnp.int32(0), jnp.int32(0)
        for k in range(moves):
            hit = arrive_slots[k] == slot
            which = jnp.where(hit, k, which)
            moved = jnp.where(hit, 1, moved)
        flag = jnp.full((page, 2 * head_dim), moved, jnp.int32) > 0
        kept = cache[slot].astype(jnp.float32)
        swapped_in = arrived[which].astype(jnp.float32)
        context[b] = jnp.where(flag, swapped_in, kept).astype(jnp.bfloat16)
        return carry

    lax.fori_loop(0, batch, gather, 0, unroll=8)

    tile_rows = group_size * ROW_TILE
    here = lax.broadcasted_iota(jnp.int32, (batch, batch), 0)
    there = lax.broadcasted_iota(jnp.int32, (batch, batch), 1)
    lengths = jnp.where(here == there, cached_length[...].astype(jnp.float32), 0.0)
    lengths = jnp.sum(lengths, axis=-1, keepdims=True)
    to_entry = lax.broadcasted_iota(jnp.int32, (ROW_TILE, 2 * ROW_TILE), 1) == (
        2 * lax.broadcasted_iota(jnp.int32, (ROW_TILE, 2 * ROW_TILE), 0) + p
    )
    to_entry = to_entry.astype(jnp.float32).astype(jnp.bfloat16)
    to_entry = jnp.concatenate([to_entry] * group_size, axis=0)
    score_scale = head_dim ** (-0.5)
    for c in range(chunks):
        base = c * ROW_TILE
        stacked = jnp.concatenate(
            [
                queries[base : base + ROW_TILE, g * head_dim : (g + 1) * head_dim]
                for g in range(group_size)
            ],
            axis=0,
        )
        block = context[base : base + ROW_TILE].reshape(ROW_TILE * page, 2 * head_dim)
        scores = (
            lax.dot_general(
                stacked,
                block[:, :head_dim],
                (((1,), (1,)), ((), ())),
                preferred_element_type=jnp.float32,
            )
            * score_scale
        )
        shape = (ROW_TILE, ROW_TILE * page)
        first = lax.broadcasted_iota(jnp.int32, shape, 0) * page
        offset = lax.broadcasted_iota(jnp.int32, shape, 1) - first
        live = (offset >= 0) & (
            offset.astype(jnp.float32) < lengths[base : base + ROW_TILE]
        )
        bias = jnp.where(live, 0.0, NEGATIVE)
        bias = jnp.concatenate([bias] * group_size, axis=0)
        scores = jnp.where(bias < 0.0, NEGATIVE, scores)
        newest = fresh[base : base + ROW_TILE].reshape(2 * ROW_TILE, 2 * head_dim)
        newest = jnp.dot(to_entry, newest, preferred_element_type=jnp.float32)
        fresh_score = (
            jnp.sum(stacked.astype(jnp.float32) * newest[:, :head_dim], axis=-1, keepdims=True)
            * score_scale
        )
        largest = jnp.maximum(jnp.max(scores, axis=-1, keepdims=True), fresh_score)
        raised = jnp.exp(scores - largest)
        fresh_raised = jnp.exp(fresh_score - largest)
        denominator = jnp.sum(raised, axis=-1, keepdims=True) + fresh_raised
        value = jnp.dot(
            raised.astype(jnp.bfloat16), block[:, head_dim:], preferred_element_type=jnp.float32
        )
        value = (value + fresh_raised * newest[:, head_dim:]) / denominator
        level = jnp.broadcast_to(largest + jnp.log(denominator), (tile_rows, head_dim))
        for s in range(pool_count):
            rows = slice(s * half_heads * ROW_TILE, (s + 1) * half_heads * ROW_TILE)
            values_out[s, c] = value[rows].astype(jnp.bfloat16)
            level_out[s, c] = level[rows]
    value_copy = send(values_out.at[partner], values_in, 0, 0, 1)
    level_copy = send(level_out.at[partner], level_in, 0, 0, 1)
    for copy in weight_copies:
        copy.wait_recv()
    own_line = weights.at[pl.ds(h * req_count, req_count)]
    weight_copies = [send(own_line, own_line, 0, kh, 0) for kh in range(1, head_count)]

    spread = lax.broadcasted_iota(jnp.int32, (batch, rows_here), 0) == (
        lax.broadcasted_iota(jnp.int32, (batch, rows_here), 1) + h * rows_here
    )
    spread = jnp.where(p == 0, spread.astype(jnp.float32), 0.0).astype(jnp.bfloat16)
    loads[3].wait()
    value_copy.wait_recv()
    level_copy.wait_recv()
    merged = []
    for c in range(chunks):
        first_level, second_level = level_out[p, c], level_in[c]
        top = jnp.maximum(first_level, second_level)
        first_share = jnp.exp(first_level - top)
        second_share = jnp.exp(second_level - top)
        value = values_out[p, c].astype(jnp.float32) * first_share
        value = value + values_in[c].astype(jnp.float32) * second_share
        value = (value / (first_share + second_share)).astype(jnp.bfloat16)
        merged.append(
            jnp.concatenate(
                [value[g * ROW_TILE : (g + 1) * ROW_TILE] for g in range(half_heads)], axis=1
            )
        )
    merged = jnp.concatenate(merged, axis=0)
    blocks = head_count * pool_count
    for d in range(blocks):
        columns = slice(d * col_block, (d + 1) * col_block)
        part = jnp.dot(merged, output_weight[:, columns], preferred_element_type=jnp.float32)
        part = part + jnp.dot(spread, residual[:, columns], preferred_element_type=jnp.float32)
        partial_out[d] = part.astype(jnp.bfloat16)
    partial_copies = []
    for kh in list(range(1, head_count)) + [0]:
        for kp in range(pool_count):
            if kh or kp:
                to_pool = partner if kp else p
                to_head = head_peer(kh) if kh else h
                partial_copies.append(
                    send(
                        partial_out.at[to_pool * head_count + to_head],
                        partial_in.at[kh * pool_count + kp],
                        0,
                        kh,
                        kp,
                    )
                )
    mine = p * head_count + h
    summed = partial_out[mine].astype(jnp.float32)
    order = [kh * pool_count + kp for kh in list(range(1, head_count)) + [0] for kp in range(pool_count) if kh or kp]
    for copy, slot in zip(partial_copies, order):
        copy.wait_recv()
        summed = summed + partial_in[slot].astype(jnp.float32)
    hidden[mine, r] = summed.astype(jnp.bfloat16)

    def hidden_block(at_head, at_req):
        return hidden.at[p * head_count + at_head, at_req]

    own_hidden = hidden_block(h, r)
    req_copies = {kr: send(own_hidden, own_hidden, kr, 0, 0) for kr in range(1, req_count)}
    head_copies, pool_copies = {}, {}
    for kh in range(1, head_count):
        head_copies[kh, 0] = send(own_hidden, own_hidden, 0, kh, 0)
    pool_copies[0, 0] = send(own_hidden, own_hidden, 0, 0, 1)
    for kr in range(1, req_count):
        req_copies[kr].wait_recv()
        block = hidden_block(h, req_source(kr))
        for kh in range(1, head_count):
            head_copies[kh, kr] = send(block, block, 0, kh, 0)
        pool_copies[0, kr] = send(block, block, 0, 0, 1)

    loads[4].wait()
    row_count = req_count * batch
    units = gate_up.shape[1]
    gate = jnp.zeros((row_count, units), jnp.float32)
    up = jnp.zeros((row_count, units), jnp.float32)
    squares = jnp.zeros((row_count, 1), jnp.float32)

    def accumulate(state, chunk):
        gate, up, squares = state
        x = hidden[chunk].reshape(row_count, col_block).astype(jnp.float32)
        columns = pl.ds(pl.multiple_of(chunk * col_block, col_block), col_block)
        scaled = (x * norm_gain[:, columns]).astype(jnp.bfloat16)
        contract = (((1,), (1,)), ((), ()))
        gate = gate + lax.dot_general(
            scaled, gate_up[0, :, columns], contract, preferred_element_type=jnp.float32
        )
        up = up + lax.dot_general(
            scaled, gate_up[1, :, columns], contract, preferred_element_type=jnp.float32
        )
        return gate, up, squares + jnp.sum(x * x, axis=-1, keepdims=True)

    state = (gate, up, squares)
    state = accumulate(state, mine)
    for kh in range(1, head_count):
        for kr in range(req_count):
            head_copies[kh, kr].wait_recv()
            block = hidden_block(head_source(kh), req_source(kr) if kr else r)
            pool_copies[kh, kr] = send(block, block, 0, 0, 1)
        state = accumulate(state, p * head_count + head_source(kh))
        for kr in range(req_count):
            pool_copies[kh - 1, kr].wait_recv()
        state = accumulate(state, partner * head_count + (head_source(kh - 1) if kh > 1 else h))
    last = head_count - 1
    for kr in range(req_count):
        pool_copies[last, kr].wait_recv()
    state = accumulate(state, partner * head_count + (head_source(last) if last else h))
    gate, up, squares = state
    scale = lax.rsqrt(squares * (1.0 / width) + 1e-06)
    gate = gate * scale
    activated = (gate / (1.0 + jnp.exp(-gate)) * (up * scale)).astype(jnp.bfloat16)
    place_row = lax.broadcasted_iota(jnp.int32, (ROW_TILE, row_count), 0)
    place_col = lax.broadcasted_iota(jnp.int32, (ROW_TILE, row_count), 1)
    for copy in weight_copies:
        copy.wait_recv()
    for to_head in range(head_count):
        placing = jnp.concatenate(
            [
                (
                    (place_row + (to_req * batch + to_head * rows_here) == place_col)
                    & (place_row < rows_here)
                )
                .astype(jnp.float32)
                .astype(jnp.bfloat16)
                for to_req in range(req_count)
            ],
            axis=0,
        )
        active[to_head] = jnp.dot(placing, activated, preferred_element_type=jnp.float32).astype(
            jnp.bfloat16
        )
    loads[5].wait()
    expert = r * head_count + h
    diagonal = lax.broadcasted_iota(jnp.int32, (ROW_TILE, weights.shape[2]), 0) == (
        lax.broadcasted_iota(jnp.int32, (ROW_TILE, weights.shape[2]), 1)
    )

    def expert_part(to_head, side):
        weight = jnp.concatenate(
            [
                jnp.where(diagonal, weights[to_head * req_count + k, pl.ds(expert, 1), :], 0.0)
                for k in range(req_count)
            ],
            axis=0,
        )
        weight = jnp.sum(weight, axis=-1, keepdims=True)
        columns = pl.ds(pl.multiple_of(side * half, half), half)
        value = jnp.dot(
            active[to_head], down_weight[:, columns], preferred_element_type=jnp.float32
        )
        return value * weight

    turn = list(range(1, head_count)) + [0]
    swap_copies = {}
    for kh in turn:
        pool_out[kh] = expert_part(head_peer(kh) if kh else h, partner).astype(jnp.bfloat16)
        swap_copies[kh] = send(pool_out.at[kh], pool_in.at[kh], 0, 0, 1)
    for kh in turn:
        own_part[kh] = expert_part(head_peer(kh) if kh else h, p)
    for kh in turn:
        swap_copies[kh].wait_recv()
        both = own_part[kh] + pool_in[kh].astype(jnp.float32)
        both = both.reshape(req_count, ROW_TILE, half)[:, :rows_here]
        if kh:
            head_out[kh - 1] = both.astype(jnp.bfloat16)
        else:
            totals[...] = both
    back_copies = {}
    for kr in list(range(1, req_count)) + [0]:
        to_req = req_peer(kr) if kr else r
        for kh in range(1, head_count):
            back_copies[kh, kr] = send(
                head_out.at[kh - 1, to_req], head_in.at[kh - 1, to_req], 0, kh, 0
            )

    def back_sum(kr):
        to_req = req_peer(kr) if kr else r
        total = totals[to_req]
        for kh in range(1, head_count):
            back_copies[kh, kr].wait_recv()
            total = total + head_in[kh - 1, to_req].astype(jnp.float32)
        return total

    last_copies = []
    for kr in range(1, req_count):
        req_out[kr - 1] = back_sum(kr).astype(jnp.bfloat16)
        last_copies.append(send(req_out.at[kr - 1], req_in.at[kr - 1], kr, 0, 0))
    pick = lax.broadcasted_iota(jnp.int32, (ROW_TILE, batch), 1) == (
        lax.broadcasted_iota(jnp.int32, (ROW_TILE, batch), 0) + h * rows_here
    )
    pick = pick.astype(jnp.float32).astype(jnp.bfloat16)
    stream = jnp.concatenate(
        [
            jnp.dot(pick, hidden[p * head_count + c, r], preferred_element_type=jnp.float32)
            for c in range(head_count)
        ],
        axis=1,
    )
    total = stream[:rows_here] + back_sum(0)
    for kr, copy in enumerate(last_copies):
        copy.wait_recv()
        total = total + req_in[kr].astype(jnp.float32)
    decoded[...] = total.astype(jnp.bfloat16)
    for copy in sent:
        copy.wait_send()


def local(*arguments):
    queries, new_entries, cache_pages, page_table = arguments[:4]
    residual, expert_choice = arguments[7], arguments[10]
    rows_here = residual.shape[0]
    expert_count = lax.axis_size("req") * lax.axis_size("head")
    capacity = max(
        2,
        min(
            rows_here,
            (2 * rows_here * expert_choice.shape[1] + expert_count - 1) // expert_count,
        ),
    )
    fits = (
        capacity == rows_here
        and rows_here <= ROW_TILE
        and expert_count <= 128
        and cache_pages.shape[0] == 1
        and page_table.shape[2] == 1
        and cache_pages.shape[2] == ROW_TILE
        and queries.shape[0] % ROW_TILE == 0
        and queries.shape[0] == rows_here * lax.axis_size("head")
        and lax.axis_size("pool") == 2
        and new_entries.shape[1] == 2
        and arguments[12].shape[0] == 1
    )
    if not fits:
        return local_routed(*arguments)
    return local_dense(*arguments)


def local_dense(
    queries,
    new_entries,
    cache_pages,
    page_table,
    cached_length,
    leave_slots,
    arrive_slots,
    residual,
    norm_gain,
    output_weight,
    expert_choice,
    route_weight,
    gate_up,
    down_weight,
):
    reqs, heads, pools = lax.axis_size("req"), lax.axis_size("head"), lax.axis_size("pool")
    batch = queries.shape[0]
    rows_here, width = residual.shape
    slots, page, entry = cache_pages.shape[1:]
    head_dim = entry // 2
    group_size = queries.shape[1] // head_dim
    moves = leave_slots.shape[0]
    fresh = new_entries.reshape(batch, -1, entry)
    col_block = width // (heads * pools)
    half = width // pools
    chunks = batch // ROW_TILE
    half_rows = group_size // pools * ROW_TILE
    group_rows = reqs * ROW_TILE
    units = gate_up.shape[2]
    copies = (
        1
        + (reqs - 1)
        + (heads - 1)
        + 2
        + (heads * pools - 1)
        + (reqs - 1)
        + reqs * (heads - 1)
        + reqs * heads
        + heads
        + (heads - 1) * reqs
        + (reqs - 1)
    )
    smem = pl.BlockSpec(memory_space=pltpu.SMEM)
    vmem = pl.BlockSpec(memory_space=pltpu.VMEM)
    hbm = pl.BlockSpec(memory_space=pl.ANY)
    narrow, full = jnp.bfloat16, jnp.float32
    return pl.pallas_call(
        functools.partial(layer_kernel, reqs, heads, pools),
        out_shape=jax.ShapeDtypeStruct((rows_here, half), narrow),
        in_specs=[smem] * 3 + [vmem] * 5 + [hbm] * 6,
        out_specs=vmem,
        scratch_shapes=[
            pltpu.VMEM(queries.shape, narrow),
            pltpu.VMEM(fresh.shape, narrow),
            pltpu.VMEM((slots, page, entry), narrow),
            pltpu.VMEM(output_weight.shape, narrow),
            pltpu.VMEM(gate_up.shape[1:], narrow),
            pltpu.VMEM(down_weight.shape[1:], narrow),
            pltpu.VMEM((moves, page, entry), narrow),
            pltpu.VMEM((moves, page, entry), narrow),
            pltpu.VMEM((batch, page, entry), narrow),
            pltpu.VMEM((heads * reqs, -(-reqs * heads // 8) * 8, 128), full),
            pltpu.VMEM((pools, chunks, half_rows, head_dim), narrow),
            pltpu.VMEM((chunks, half_rows, head_dim), narrow),
            pltpu.VMEM((pools, chunks, half_rows, head_dim), full),
            pltpu.VMEM((chunks, half_rows, head_dim), full),
            pltpu.VMEM((heads * pools, batch, col_block), narrow),
            pltpu.VMEM((heads * pools, batch, col_block), narrow),
            pltpu.VMEM((heads * pools, reqs, batch, col_block), narrow),
            pltpu.VMEM((heads, group_rows, units), narrow),
            pltpu.VMEM((heads, group_rows, half), full),
            pltpu.VMEM((heads, group_rows, half), narrow),
            pltpu.VMEM((heads, group_rows, half), narrow),
            pltpu.VMEM((heads - 1, reqs, rows_here, half), narrow),
            pltpu.VMEM((heads - 1, reqs, rows_here, half), narrow),
            pltpu.VMEM((reqs, rows_here, half), full),
            pltpu.VMEM((reqs - 1, rows_here, half), narrow),
            pltpu.VMEM((reqs - 1, rows_here, half), narrow),
            pltpu.SemaphoreType.DMA((6,)),
            pltpu.SemaphoreType.DMA((copies,)),
            pltpu.SemaphoreType.DMA((copies,)),
        ],
        compiler_params=pltpu.CompilerParams(
            collective_id=0, has_side_effects=True, vmem_limit_bytes=56 * 1024 * 1024
        ),
        name="layer",
    )(
        page_table.reshape(-1),
        leave_slots,
        arrive_slots,
        cached_length.T,
        expert_choice.T,
        route_weight.T,
        residual,
        norm_gain.reshape(1, -1),
        queries,
        fresh,
        cache_pages,
        output_weight,
        gate_up,
        down_weight,
    )


def solution(mesh):
    return jax.shard_map(
        local,
        mesh=mesh,
        in_specs=(
            P(("group", "req"), "head"),
            P(("group", "req"), None, "head", None),
            P("head", ("group", "req", "pool"), None, None),
            P(("group", "req"), "pool", None),
            P(("group", "req"), "pool"),
            P(("group", "req", "pool")),
            P(("group", "req", "pool")),
            P(("group", "req", "head"), None),
            P(),
            P(("head", "pool"), None),
            P(("group", "req", "head"), None),
            P(("group", "req", "head"), None),
            P(("req", "head"), None, "pool", None),
            P(("req", "head"), "pool", None),
        ),
        out_specs=P(("group", "req", "head"), "pool"),
        check_vma=False,
    )
```

```python
import functools

import jax
import jax.numpy as jnp
from jax import lax
from jax.experimental import pallas as pl
from jax.experimental.pallas import tpu as pltpu
from jax.sharding import PartitionSpec as P

MESH = pl.DeviceIdType.MESH
ROW_TILE = 16
NEGATIVE = -1e30


def swapped(value, axis, apart):
    mask = 2**apart
    pairs = [(source, source ^ mask) for source in range(lax.axis_size(axis))]
    return lax.ppermute(value, axis, pairs)


def combined_all(shard, axis, join):
    gathered = jax.tree.map(
        lambda a, kind: lax.all_gather(a.astype(kind), axis),
        shard,
        (jnp.bfloat16, jnp.bfloat16, jnp.bfloat16),
    )

    def take(source):
        return jax.tree.map(
            lambda a, own: lax.dynamic_index_in_dim(a, source, 0, False).astype(own.dtype),
            gathered,
            shard,
        )

    return lax.fori_loop(
        1, lax.axis_size(axis), lambda source, state: join(state, take(source)), take(0)
    )


def merge_parts(earlier, later):
    first_max, first_denominator, first_value = earlier
    second_max, second_denominator, second_value = later
    largest = jnp.maximum(first_max, second_max)
    first_scale = jnp.exp(first_max - largest)
    second_scale = jnp.exp(second_max - largest)
    denominator = first_denominator * first_scale + second_denominator * second_scale
    weighted = first_value * first_scale[..., None] + second_value * second_scale[..., None]
    return (largest, denominator, weighted)


def local_routed(
    queries,
    new_entries,
    cache_pages,
    page_table,
    cached_length,
    leave_slots,
    arrive_slots,
    residual,
    norm_gain,
    output_weight,
    expert_choice,
    route_weight,
    gate_up,
    down_weight,
):
    batch_size = queries.shape[0]
    group_count = cache_pages.shape[0]
    head_dim = new_entries.shape[3] // 2
    group_size = queries.shape[1] // (group_count * head_dim)
    pool_index = lax.axis_index("pool")
    outgoing = cache_pages[:, leave_slots]
    arrived = swapped(outgoing, "pool", 0)
    current = cache_pages.at[:, arrive_slots].set(arrived)
    context = current[:, page_table[:, 0, :]]
    context = context.reshape(group_count, batch_size, -1, 2 * head_dim)
    context_keys = context[..., :head_dim]
    context_values = context[..., head_dim:]
    grouped_queries = queries.reshape(batch_size, group_count, group_size, head_dim)
    score_scale = head_dim ** (-0.5)
    attention_scores = (
        jnp.einsum(
            "bgqd,gbtd->bgqt", grouped_queries, context_keys, preferred_element_type=jnp.float32
        )
        * score_scale
    )
    positions = jnp.arange(context.shape[2], dtype=jnp.int32)
    valid_mask = positions[None, :] < cached_length
    attention_scores = jnp.where(valid_mask[:, None, None, :], attention_scores, -jnp.inf)
    fresh_scores = (
        jnp.einsum(
            "bgqd,bsgd->bgqs",
            grouped_queries,
            new_entries[..., :head_dim],
            preferred_element_type=jnp.float32,
        )
        * score_scale
    )
    fresh_scores = jnp.where(pool_index == 0, fresh_scores, -jnp.inf)
    largest = jnp.maximum(jnp.max(attention_scores, axis=-1), jnp.max(fresh_scores, axis=-1))
    local_weights = jnp.exp(attention_scores - largest[..., None])
    fresh_weights = jnp.exp(fresh_scores - largest[..., None])
    denominator = jnp.sum(local_weights, axis=-1) + jnp.sum(fresh_weights, axis=-1)
    weighted = jnp.einsum("bgqt,gbtd->bgqd", local_weights, context_values.astype(jnp.float32))
    weighted = weighted + jnp.einsum(
        "bgqs,bsgd->bgqd", fresh_weights, new_entries[..., head_dim:].astype(jnp.float32)
    )
    largest, denominator, weighted = combined_all(
        (largest, denominator, weighted), "pool", merge_parts
    )
    attended = (weighted / denominator[..., None]).reshape(batch_size, -1).astype(jnp.bfloat16)
    head_width = output_weight.shape[0]
    own_heads = lax.dynamic_slice_in_dim(attended, pool_index * head_width, head_width, 1)
    partial_value = jnp.dot(own_heads, output_weight, preferred_element_type=jnp.float32)
    rows_here = residual.shape[0]
    summed = lax.psum(partial_value.astype(jnp.bfloat16), ("head", "pool")).astype(jnp.float32)
    attention = lax.dynamic_slice_in_dim(summed, lax.axis_index("head") * rows_here, rows_here, 0)
    hidden = residual.astype(jnp.float32) + attention
    normed = (
        hidden * lax.rsqrt(jnp.mean(hidden * hidden, axis=-1, keepdims=True) + 1e-06) * norm_gain
    ).astype(jnp.bfloat16)
    expert_count = lax.axis_size("req") * lax.axis_size("head")
    top_count = expert_choice.shape[1]
    capacity = max(
        2, min(rows_here, (2 * rows_here * top_count + expert_count - 1) // expert_count)
    )
    flat_choice = expert_choice.reshape(-1)
    expert_hits = (
        flat_choice[:, None] == jnp.arange(expert_count, dtype=jnp.int32)[None, :]
    ).astype(jnp.int32)
    earlier = jnp.cumsum(expert_hits, axis=0) - expert_hits
    slot_index = jnp.sum(earlier * expert_hits, axis=1)
    target = flat_choice * capacity + slot_index
    placed = (
        target[:, None] == jnp.arange(expert_count * capacity, dtype=jnp.int32)[None, :]
    ).astype(jnp.float32)
    placed = placed.reshape(rows_here, top_count, expert_count * capacity)
    dispatch = jnp.sum(placed, axis=1).astype(jnp.bfloat16)
    combine_matrix = jnp.sum(placed * route_weight[:, :, None], axis=1)
    outgoing_rows = jnp.einsum("re,rd->ed", dispatch, normed, preferred_element_type=jnp.float32)
    outgoing_rows = outgoing_rows.astype(jnp.bfloat16).reshape(expert_count, capacity, -1)
    model_width = normed.shape[1]
    half_width = model_width // lax.axis_size("pool")
    projection = gate_up[0].reshape(-1, model_width)
    hidden_size = projection.shape[0] // 2
    received = lax.all_to_all(
        outgoing_rows, ("req", "head"), split_axis=0, concat_axis=0, tiled=True
    )
    sources = received.shape[0]
    item_count = received.shape[1]
    flat_rows = received.reshape(sources * item_count, model_width)
    projected = jnp.einsum("nd,fd->nf", flat_rows, projection, preferred_element_type=jnp.float32)
    activated = (jax.nn.silu(projected[:, :hidden_size]) * projected[:, hidden_size:]).astype(
        jnp.bfloat16
    )
    part_sum = jnp.dot(activated, down_weight[0], preferred_element_type=jnp.float32).reshape(
        sources, item_count, model_width
    )
    column_sum = lax.psum_scatter(
        part_sum.astype(jnp.bfloat16), "pool", scatter_dimension=2, tiled=True
    )
    returned = lax.all_to_all(column_sum, ("req", "head"), split_axis=0, concat_axis=0, tiled=True)
    gathered = returned.reshape(expert_count * capacity, half_width).astype(jnp.float32)
    expert_mix = jnp.dot(combine_matrix, gathered, precision=lax.Precision.HIGHEST)
    own_columns = lax.dynamic_slice_in_dim(hidden, pool_index * half_width, half_width, 1)
    return (own_columns + expert_mix).astype(jnp.bfloat16)


def layer_kernel(
    req_count,
    head_count,
    pool_count,
    page_table,
    leave_slots,
    arrive_slots,
    cached_length,
    expert_choice,
    route_weight,
    residual,
    norm_gain,
    queries_hbm,
    fresh_hbm,
    cache_hbm,
    output_weight_hbm,
    gate_up_hbm,
    down_weight_hbm,
    decoded,
    queries,
    fresh,
    cache,
    output_weight,
    gate_up,
    down_weight,
    leaving,
    arrived,
    context,
    weights,
    values_out,
    values_in,
    level_out,
    level_in,
    partial_out,
    partial_in,
    hidden,
    active,
    own_part,
    pool_out,
    pool_in,
    head_out,
    head_in,
    totals,
    req_out,
    req_in,
    load_sem,
    send_sem,
    recv_sem,
):
    r, h, p = lax.axis_index("req"), lax.axis_index("head"), lax.axis_index("pool")
    batch, page = queries.shape[0], cache.shape[1]
    head_dim = cache.shape[2] // 2
    group_size = queries.shape[1] // head_dim
    rows_here = residual.shape[0]
    width = residual.shape[1]
    col_block = width // (head_count * pool_count)
    half = width // pool_count
    half_heads = group_size // pool_count
    chunks = batch // ROW_TILE
    moves = leaving.shape[0]

    loads = [
        pltpu.make_async_copy(source, target, load_sem.at[i])
        for i, (source, target) in enumerate(
            (
                (cache_hbm.at[0], cache),
                (queries_hbm, queries),
                (fresh_hbm, fresh),
                (output_weight_hbm, output_weight),
                (gate_up_hbm.at[0], gate_up),
                (down_weight_hbm.at[0], down_weight),
            )
        )
    ]
    for load in loads:
        load.start()

    def req_peer(k):
        return lax.rem(r + k, req_count)

    def head_peer(k):
        return lax.rem(h + k, head_count)

    def req_source(k):
        return lax.rem(r + req_count - k, req_count)

    def head_source(k):
        return lax.rem(h + head_count - k, head_count)

    partner = 1 - p
    barrier = pltpu.get_barrier_semaphore()
    peers = [
        (kr, kh, kp)
        for kr in range(req_count)
        for kh in range(head_count)
        for kp in range(pool_count)
        if (kr, kh, kp) != (0, 0, 0) and (kr > 0) + (kh > 0) + (kp > 0) == 1
    ]

    def where_is(kr, kh, kp):
        return {
            "req": req_peer(kr) if kr else r,
            "head": head_peer(kh) if kh else h,
            "pool": partner if kp else p,
        }

    for peer in peers:
        pl.semaphore_signal(barrier, inc=1, device_id=where_is(*peer), device_id_type=MESH)

    experts = weights.shape[1]
    named = lax.broadcasted_iota(jnp.int32, (experts, rows_here), 0)
    dense = jnp.zeros((experts, rows_here), jnp.float32)
    for k in range(expert_choice.shape[0]):
        dense = dense + jnp.where(named == expert_choice[k : k + 1, :], route_weight[k : k + 1, :], 0.0)
    own_block = h * req_count + r
    weights[own_block] = jnp.concatenate(
        [dense, jnp.zeros((experts, weights.shape[2] - rows_here), jnp.float32)], axis=1
    )

    sent = []

    def send(source, target, kr, kh, kp):
        at = len(sent)
        copy = pltpu.make_async_remote_copy(
            src_ref=source,
            dst_ref=target,
            send_sem=send_sem.at[at],
            recv_sem=recv_sem.at[at],
            device_id=where_is(kr, kh, kp),
            device_id_type=MESH,
        )
        copy.start()
        sent.append(copy)
        return copy

    loads[0].wait()
    for k in range(moves):
        leaving[k] = cache[leave_slots[k]]
    pl.semaphore_wait(barrier, len(peers))
    pages = send(leaving, arrived, 0, 0, 1)
    weight_copies = [
        send(weights.at[own_block], weights.at[own_block], kr, 0, 0) for kr in range(1, req_count)
    ]
    loads[1].wait()
    loads[2].wait()
    pages.wait_recv()

    def gather(b, carry):
        slot = page_table[b]
        which, moved = jnp.int32(0), jnp.int32(0)
        for k in range(moves):
            hit = arrive_slots[k] == slot
            which = jnp.where(hit, k, which)
            moved = jnp.where(hit, 1, moved)
        flag = jnp.full((page, 2 * head_dim), moved, jnp.int32) > 0
        kept = cache[slot].astype(jnp.float32)
        swapped_in = arrived[which].astype(jnp.float32)
        context[b] = jnp.where(flag, swapped_in, kept).astype(jnp.bfloat16)
        return carry

    lax.fori_loop(0, batch, gather, 0, unroll=8)

    tile_rows = group_size * ROW_TILE
    here = lax.broadcasted_iota(jnp.int32, (batch, batch), 0)
    there = lax.broadcasted_iota(jnp.int32, (batch, batch), 1)
    lengths = jnp.where(here == there, cached_length[...].astype(jnp.float32), 0.0)
    lengths = jnp.sum(lengths, axis=-1, keepdims=True)
    to_entry = lax.broadcasted_iota(jnp.int32, (ROW_TILE, 2 * ROW_TILE), 1) == (
        2 * lax.broadcasted_iota(jnp.int32, (ROW_TILE, 2 * ROW_TILE), 0) + p
    )
    to_entry = to_entry.astype(jnp.float32).astype(jnp.bfloat16)
    to_entry = jnp.concatenate([to_entry] * group_size, axis=0)
    score_scale = head_dim ** (-0.5)
    for c in range(chunks):
        base = c * ROW_TILE
        stacked = jnp.concatenate(
            [
                queries[base : base + ROW_TILE, g * head_dim : (g + 1) * head_dim]
                for g in range(group_size)
            ],
            axis=0,
        )
        block = context[base : base + ROW_TILE].reshape(ROW_TILE * page, 2 * head_dim)
        scores = (
            lax.dot_general(
                stacked,
                block[:, :head_dim],
                (((1,), (1,)), ((), ())),
                preferred_element_type=jnp.float32,
            )
            * score_scale
        )
        shape = (ROW_TILE, ROW_TILE * page)
        first = lax.broadcasted_iota(jnp.int32, shape, 0) * page
        offset = lax.broadcasted_iota(jnp.int32, shape, 1) - first
        live = (offset >= 0) & (
            offset.astype(jnp.float32) < lengths[base : base + ROW_TILE]
        )
        bias = jnp.where(live, 0.0, NEGATIVE)
        bias = jnp.concatenate([bias] * group_size, axis=0)
        scores = jnp.where(bias < 0.0, NEGATIVE, scores)
        newest = fresh[base : base + ROW_TILE].reshape(2 * ROW_TILE, 2 * head_dim)
        newest = jnp.dot(to_entry, newest, preferred_element_type=jnp.float32)
        fresh_score = (
            jnp.sum(stacked.astype(jnp.float32) * newest[:, :head_dim], axis=-1, keepdims=True)
            * score_scale
        )
        largest = jnp.maximum(jnp.max(scores, axis=-1, keepdims=True), fresh_score)
        raised = jnp.exp(scores - largest)
        fresh_raised = jnp.exp(fresh_score - largest)
        denominator = jnp.sum(raised, axis=-1, keepdims=True) + fresh_raised
        value = jnp.dot(
            raised.astype(jnp.bfloat16), block[:, head_dim:], preferred_element_type=jnp.float32
        )
        value = (value + fresh_raised * newest[:, head_dim:]) / denominator
        level = jnp.broadcast_to(largest + jnp.log(denominator), (tile_rows, head_dim))
        for s in range(pool_count):
            rows = slice(s * half_heads * ROW_TILE, (s + 1) * half_heads * ROW_TILE)
            values_out[s, c] = value[rows].astype(jnp.bfloat16)
            level_out[s, c] = level[rows]
    value_copy = send(values_out.at[partner], values_in, 0, 0, 1)
    level_copy = send(level_out.at[partner], level_in, 0, 0, 1)
    for copy in weight_copies:
        copy.wait_recv()
    own_line = weights.at[pl.ds(h * req_count, req_count)]
    weight_copies = [send(own_line, own_line, 0, kh, 0) for kh in range(1, head_count)]

    spread = lax.broadcasted_iota(jnp.int32, (batch, rows_here), 0) == (
        lax.broadcasted_iota(jnp.int32, (batch, rows_here), 1) + h * rows_here
    )
    spread = jnp.where(p == 0, spread.astype(jnp.float32), 0.0).astype(jnp.bfloat16)
    loads[3].wait()
    value_copy.wait_recv()
    level_copy.wait_recv()
    merged = []
    for c in range(chunks):
        first_level, second_level = level_out[p, c], level_in[c]
        top = jnp.maximum(first_level, second_level)
        first_share = jnp.exp(first_level - top)
        second_share = jnp.exp(second_level - top)
        value = values_out[p, c].astype(jnp.float32) * first_share
        value = value + values_in[c].astype(jnp.float32) * second_share
        value = (value / (first_share + second_share)).astype(jnp.bfloat16)
        merged.append(
            jnp.concatenate(
                [value[g * ROW_TILE : (g + 1) * ROW_TILE] for g in range(half_heads)], axis=1
            )
        )
    merged = jnp.concatenate(merged, axis=0)
    blocks = head_count * pool_count
    for d in range(blocks):
        columns = slice(d * col_block, (d + 1) * col_block)
        part = jnp.dot(merged, output_weight[:, columns], preferred_element_type=jnp.float32)
        part = part + jnp.dot(spread, residual[:, columns], preferred_element_type=jnp.float32)
        partial_out[d] = part.astype(jnp.bfloat16)
    partial_copies = []
    for kh in list(range(1, head_count)) + [0]:
        for kp in range(pool_count):
            if kh or kp:
                to_pool = partner if kp else p
                to_head = head_peer(kh) if kh else h
                partial_copies.append(
                    send(
                        partial_out.at[to_pool * head_count + to_head],
                        partial_in.at[kh * pool_count + kp],
                        0,
                        kh,
                        kp,
                    )
                )
    mine = p * head_count + h
    summed = partial_out[mine].astype(jnp.float32)
    order = [kh * pool_count + kp for kh in list(range(1, head_count)) + [0] for kp in range(pool_count) if kh or kp]
    for copy, slot in zip(partial_copies, order):
        copy.wait_recv()
        summed = summed + partial_in[slot].astype(jnp.float32)
    hidden[mine, r] = summed.astype(jnp.bfloat16)

    def hidden_block(at_head, at_req):
        return hidden.at[p * head_count + at_head, at_req]

    own_hidden = hidden_block(h, r)
    req_copies = {kr: send(own_hidden, own_hidden, kr, 0, 0) for kr in range(1, req_count)}
    head_copies, pool_copies = {}, {}
    for kh in range(1, head_count):
        head_copies[kh, 0] = send(own_hidden, own_hidden, 0, kh, 0)
    pool_copies[0, 0] = send(own_hidden, own_hidden, 0, 0, 1)
    for kr in sorted(range(1, req_count), key=lambda k: min(k, req_count - k)):
        req_copies[kr].wait_recv()
        block = hidden_block(h, req_source(kr))
        for kh in range(1, head_count):
            head_copies[kh, kr] = send(block, block, 0, kh, 0)
        pool_copies[0, kr] = send(block, block, 0, 0, 1)

    loads[4].wait()
    row_count = req_count * batch
    units = gate_up.shape[1]
    gate = jnp.zeros((row_count, units), jnp.float32)
    up = jnp.zeros((row_count, units), jnp.float32)
    squares = jnp.zeros((row_count, 1), jnp.float32)

    def accumulate(state, chunk):
        gate, up, squares = state
        x = hidden[chunk].reshape(row_count, col_block).astype(jnp.float32)
        columns = pl.ds(pl.multiple_of(chunk * col_block, col_block), col_block)
        scaled = (x * norm_gain[:, columns]).astype(jnp.bfloat16)
        contract = (((1,), (1,)), ((), ()))
        gate = gate + lax.dot_general(
            scaled, gate_up[0, :, columns], contract, preferred_element_type=jnp.float32
        )
        up = up + lax.dot_general(
            scaled, gate_up[1, :, columns], contract, preferred_element_type=jnp.float32
        )
        return gate, up, squares + jnp.sum(x * x, axis=-1, keepdims=True)

    state = (gate, up, squares)
    state = accumulate(state, mine)
    for kh in range(1, head_count):
        for kr in range(req_count):
            head_copies[kh, kr].wait_recv()
            block = hidden_block(head_source(kh), req_source(kr) if kr else r)
            pool_copies[kh, kr] = send(block, block, 0, 0, 1)
        state = accumulate(state, p * head_count + head_source(kh))
        for kr in range(req_count):
            pool_copies[kh - 1, kr].wait_recv()
        state = accumulate(state, partner * head_count + (head_source(kh - 1) if kh > 1 else h))
    last = head_count - 1
    for kr in range(req_count):
        pool_copies[last, kr].wait_recv()
    state = accumulate(state, partner * head_count + (head_source(last) if last else h))
    gate, up, squares = state
    scale = lax.rsqrt(squares * (1.0 / width) + 1e-06)
    gate = gate * scale
    activated = (gate / (1.0 + jnp.exp(-gate)) * (up * scale)).astype(jnp.bfloat16)
    place_row = lax.broadcasted_iota(jnp.int32, (ROW_TILE, row_count), 0)
    place_col = lax.broadcasted_iota(jnp.int32, (ROW_TILE, row_count), 1)
    for copy in weight_copies:
        copy.wait_recv()
    for to_head in range(head_count):
        placing = jnp.concatenate(
            [
                (
                    (place_row + (to_req * batch + to_head * rows_here) == place_col)
                    & (place_row < rows_here)
                )
                .astype(jnp.float32)
                .astype(jnp.bfloat16)
                for to_req in range(req_count)
            ],
            axis=0,
        )
        active[to_head] = jnp.dot(placing, activated, preferred_element_type=jnp.float32).astype(
            jnp.bfloat16
        )
    loads[5].wait()
    expert = r * head_count + h
    diagonal = lax.broadcasted_iota(jnp.int32, (ROW_TILE, weights.shape[2]), 0) == (
        lax.broadcasted_iota(jnp.int32, (ROW_TILE, weights.shape[2]), 1)
    )

    def expert_part(to_head, side):
        weight = jnp.concatenate(
            [
                jnp.where(diagonal, weights[to_head * req_count + k, pl.ds(expert, 1), :], 0.0)
                for k in range(req_count)
            ],
            axis=0,
        )
        weight = jnp.sum(weight, axis=-1, keepdims=True)
        columns = pl.ds(pl.multiple_of(side * half, half), half)
        value = jnp.dot(
            active[to_head], down_weight[:, columns], preferred_element_type=jnp.float32
        )
        return value * weight

    turn = list(range(1, head_count)) + [0]
    swap_copies = {}
    for kh in turn:
        pool_out[kh] = expert_part(head_peer(kh) if kh else h, partner).astype(jnp.bfloat16)
        swap_copies[kh] = send(pool_out.at[kh], pool_in.at[kh], 0, 0, 1)
    for kh in turn:
        own_part[kh] = expert_part(head_peer(kh) if kh else h, p)
    for kh in turn:
        swap_copies[kh].wait_recv()
        both = own_part[kh] + pool_in[kh].astype(jnp.float32)
        both = both.reshape(req_count, ROW_TILE, half)[:, :rows_here]
        if kh:
            head_out[kh - 1] = both.astype(jnp.bfloat16)
        else:
            totals[...] = both
    back_copies = {}
    for kr in list(range(1, req_count)) + [0]:
        to_req = req_peer(kr) if kr else r
        for kh in range(1, head_count):
            back_copies[kh, kr] = send(
                head_out.at[kh - 1, to_req], head_in.at[kh - 1, to_req], 0, kh, 0
            )

    def back_sum(kr):
        to_req = req_peer(kr) if kr else r
        total = totals[to_req]
        for kh in range(1, head_count):
            back_copies[kh, kr].wait_recv()
            total = total + head_in[kh - 1, to_req].astype(jnp.float32)
        return total

    last_copies = []
    for kr in range(1, req_count):
        req_out[kr - 1] = back_sum(kr).astype(jnp.bfloat16)
        last_copies.append(send(req_out.at[kr - 1], req_in.at[kr - 1], kr, 0, 0))
    pick = lax.broadcasted_iota(jnp.int32, (ROW_TILE, batch), 1) == (
        lax.broadcasted_iota(jnp.int32, (ROW_TILE, batch), 0) + h * rows_here
    )
    pick = pick.astype(jnp.float32).astype(jnp.bfloat16)
    stream = jnp.concatenate(
        [
            jnp.dot(pick, hidden[p * head_count + c, r], preferred_element_type=jnp.float32)
            for c in range(head_count)
        ],
        axis=1,
    )
    total = stream[:rows_here] + back_sum(0)
    for kr, copy in enumerate(last_copies):
        copy.wait_recv()
        total = total + req_in[kr].astype(jnp.float32)
    decoded[...] = total.astype(jnp.bfloat16)
    for copy in sent:
        copy.wait_send()


def local(*arguments):
    queries, new_entries, cache_pages, page_table = arguments[:4]
    residual, expert_choice = arguments[7], arguments[10]
    rows_here = residual.shape[0]
    expert_count = lax.axis_size("req") * lax.axis_size("head")
    capacity = max(
        2,
        min(
            rows_here,
            (2 * rows_here * expert_choice.shape[1] + expert_count - 1) // expert_count,
        ),
    )
    fits = (
        capacity == rows_here
        and rows_here <= ROW_TILE
        and expert_count <= 128
        and cache_pages.shape[0] == 1
        and page_table.shape[2] == 1
        and cache_pages.shape[2] == ROW_TILE
        and queries.shape[0] % ROW_TILE == 0
        and queries.shape[0] == rows_here * lax.axis_size("head")
        and lax.axis_size("pool") == 2
        and new_entries.shape[1] == 2
        and arguments[12].shape[0] == 1
    )
    if not fits:
        return local_routed(*arguments)
    return local_dense(*arguments)


def local_dense(
    queries,
    new_entries,
    cache_pages,
    page_table,
    cached_length,
    leave_slots,
    arrive_slots,
    residual,
    norm_gain,
    output_weight,
    expert_choice,
    route_weight,
    gate_up,
    down_weight,
):
    reqs, heads, pools = lax.axis_size("req"), lax.axis_size("head"), lax.axis_size("pool")
    batch = queries.shape[0]
    rows_here, width = residual.shape
    slots, page, entry = cache_pages.shape[1:]
    head_dim = entry // 2
    group_size = queries.shape[1] // head_dim
    moves = leave_slots.shape[0]
    fresh = new_entries.reshape(batch, -1, entry)
    col_block = width // (heads * pools)
    half = width // pools
    chunks = batch // ROW_TILE
    half_rows = group_size // pools * ROW_TILE
    group_rows = reqs * ROW_TILE
    units = gate_up.shape[2]
    copies = (
        1
        + (reqs - 1)
        + (heads - 1)
        + 2
        + (heads * pools - 1)
        + (reqs - 1)
        + reqs * (heads - 1)
        + reqs * heads
        + heads
        + (heads - 1) * reqs
        + (reqs - 1)
    )
    smem = pl.BlockSpec(memory_space=pltpu.SMEM)
    vmem = pl.BlockSpec(memory_space=pltpu.VMEM)
    hbm = pl.BlockSpec(memory_space=pl.ANY)
    narrow, full = jnp.bfloat16, jnp.float32
    return pl.pallas_call(
        functools.partial(layer_kernel, reqs, heads, pools),
        out_shape=jax.ShapeDtypeStruct((rows_here, half), narrow),
        in_specs=[smem] * 3 + [vmem] * 5 + [hbm] * 6,
        out_specs=vmem,
        scratch_shapes=[
            pltpu.VMEM(queries.shape, narrow),
            pltpu.VMEM(fresh.shape, narrow),
            pltpu.VMEM((slots, page, entry), narrow),
            pltpu.VMEM(output_weight.shape, narrow),
            pltpu.VMEM(gate_up.shape[1:], narrow),
            pltpu.VMEM(down_weight.shape[1:], narrow),
            pltpu.VMEM((moves, page, entry), narrow),
            pltpu.VMEM((moves, page, entry), narrow),
            pltpu.VMEM((batch, page, entry), narrow),
            pltpu.VMEM((heads * reqs, -(-reqs * heads // 8) * 8, 128), full),
            pltpu.VMEM((pools, chunks, half_rows, head_dim), narrow),
            pltpu.VMEM((chunks, half_rows, head_dim), narrow),
            pltpu.VMEM((pools, chunks, half_rows, head_dim), full),
            pltpu.VMEM((chunks, half_rows, head_dim), full),
            pltpu.VMEM((heads * pools, batch, col_block), narrow),
            pltpu.VMEM((heads * pools, batch, col_block), narrow),
            pltpu.VMEM((heads * pools, reqs, batch, col_block), narrow),
            pltpu.VMEM((heads, group_rows, units), narrow),
            pltpu.VMEM((heads, group_rows, half), full),
            pltpu.VMEM((heads, group_rows, half), narrow),
            pltpu.VMEM((heads, group_rows, half), narrow),
            pltpu.VMEM((heads - 1, reqs, rows_here, half), narrow),
            pltpu.VMEM((heads - 1, reqs, rows_here, half), narrow),
            pltpu.VMEM((reqs, rows_here, half), full),
            pltpu.VMEM((reqs - 1, rows_here, half), narrow),
            pltpu.VMEM((reqs - 1, rows_here, half), narrow),
            pltpu.SemaphoreType.DMA((6,)),
            pltpu.SemaphoreType.DMA((copies,)),
            pltpu.SemaphoreType.DMA((copies,)),
        ],
        compiler_params=pltpu.CompilerParams(
            collective_id=0, has_side_effects=True, vmem_limit_bytes=56 * 1024 * 1024
        ),
        name="layer",
    )(
        page_table.reshape(-1),
        leave_slots,
        arrive_slots,
        cached_length.T,
        expert_choice.T,
        route_weight.T,
        residual,
        norm_gain.reshape(1, -1),
        queries,
        fresh,
        cache_pages,
        output_weight,
        gate_up,
        down_weight,
    )


def solution(mesh):
    return jax.shard_map(
        local,
        mesh=mesh,
        in_specs=(
            P(("group", "req"), "head"),
            P(("group", "req"), None, "head", None),
            P("head", ("group", "req", "pool"), None, None),
            P(("group", "req"), "pool", None),
            P(("group", "req"), "pool"),
            P(("group", "req", "pool")),
            P(("group", "req", "pool")),
            P(("group", "req", "head"), None),
            P(),
            P(("head", "pool"), None),
            P(("group", "req", "head"), None),
            P(("group", "req", "head"), None),
            P(("req", "head"), None, "pool", None),
            P(("req", "head"), "pool", None),
        ),
        out_specs=P(("group", "req", "head"), "pool"),
        check_vma=False,
    )
```
